32 devices in a mesh: seq: 8 (over y, x, core), ch: 4 (over z).
Axes of the slice: x: 2, y: 2, z: 4, core: 2. Of those that a mesh axis runs over, the one named last changes fastest.
Arguments:
- projected: float32 [3, 512, 4096], P(None, 'ch', 'seq'), may hold values from -6 to 6
- short_taps: float32 [7, 3, 512], P(None, None, 'ch'), may hold values from -2 to 2
- medium_taps: float32 [128, 512], P(None, 'ch'), may hold values from -0.5 to 0.5
- global_kernel_taps: float32 [512, 4096], P('ch', 'seq')
- residual_coefficient: float32 [512], P('ch'), may hold values from -4 to 4
- mixer_weight: bfloat16 [512, 512], P(None, 'ch'), may hold values from -0.25 to 0.25
Outputs:
- mixed: float32 [512, 4096], P('ch', 'seq')
The draws below stay inside these ranges and needn't reach their ends.
All inputs are finite; a program needn't handle non-finite values.
Results may differ from the reference program's by a relative error of at most 0.0029.
Values may be sent and summed in bfloat16 or wider, within the bound.
A program may use at most 128 MiB of HBM per device.

```python
import math
import jax
import jax.numpy as jnp

SHORT = 7
MEDIUM = 128
C = 512
L = 4096


def draw_global_kernel_taps(key, part):
    key_rate, key_noise = jax.random.split(jax.random.fold_in(key, 17))
    rates = jnp.exp(jax.random.uniform(key_rate, (C, 1), jnp.float32, math.log(0.5), math.log(8.0)))
    times = jnp.arange(L, dtype=jnp.float32)[None, :]
    noise = jnp.clip(jax.random.normal(key_noise, (C, L), jnp.float32), -5.0, 5.0)
    return noise * jnp.sqrt(2.0 * rates / L) * jnp.exp(-rates * times / L)


def block_scale(own_key, dims, cuts, smallest, high):
    def one(position, parts):
        draws = jax.random.uniform(jax.random.fold_in(jax.random.fold_in(own_key, 6), position), (parts,), jnp.float32, smallest / len(cuts), high / len(cuts))
        return jnp.repeat(jnp.exp(draws), dims[position] // parts).reshape((-1,) + (1,) * (len(dims) - position - 1))

    gain = one(*cuts[0])
    for cut in cuts[1:]:
        gain = gain * one(*cut)
    return gain


def scatter_about(own_key, dims, spread, bound, pieces=(), kind=jnp.bfloat16):
    drawn = spread * jax.random.normal(own_key, dims, jnp.float32)
    if pieces:
        drawn = drawn * block_scale(own_key, dims, pieces, -0.22, 0.18)
    return jnp.clip(drawn, -bound, bound).astype(kind)


def setup_inputs(seed: int = 0) -> dict:
    streams_of = jax.random.split(jax.random.key(seed), 7)
    projected = scatter_about(streams_of[0], (3, C, L), 1.0, 6.0, ((1, 4), (2, 8)), jnp.float32)
    short_taps = scatter_about(streams_of[1], (SHORT, 3, C), SHORT ** -0.5, 2.0, ((2, 4),), jnp.float32)
    medium_taps = scatter_about(streams_of[2], (MEDIUM, C), MEDIUM ** -0.5, 0.5, ((1, 4),), jnp.float32)
    global_kernel_taps = draw_global_kernel_taps(jax.random.fold_in(streams_of[6], 71), 0)
    residual_coefficient = scatter_about(streams_of[4], (C,), 1.0, 4.0, ((0, 4),), jnp.float32)
    mixer_weight = scatter_about(streams_of[5], (C, C), C ** -0.5, 0.25, ((1, 4),))
    return {"projected": projected, "short_taps": short_taps, "medium_taps": medium_taps, "global_kernel_taps": global_kernel_taps, "residual_coefficient": residual_coefficient, "mixer_weight": mixer_weight}


def causal(signal, filter_taps, span_out):
    tap_count = filter_taps.shape[0]
    padded = jnp.pad(signal, [(0, 0)] * (signal.ndim - 1) + [(tap_count - 1, 0)])
    summed = jnp.zeros(signal.shape[:-1] + (span_out,), jnp.float32)
    for offset in range(tap_count):
        begin_at = tap_count - 1 - offset
        summed = summed + filter_taps[offset][..., None] * padded[..., begin_at:begin_at + span_out]
    return summed


def reference(projected, short_taps, medium_taps, global_kernel_taps, residual_coefficient, mixer_weight):
    context_extent = projected.shape[2]
    embedded_tokens = causal(projected, short_taps, context_extent)
    averaged_sequence = causal(embedded_tokens[2], medium_taps, context_extent)
    modulating_sequence = embedded_tokens[1] * averaged_sequence
    fourier_coefficients = jnp.fft.rfft(modulating_sequence, n=2 * context_extent, axis=1) * jnp.fft.rfft(global_kernel_taps, n=2 * context_extent, axis=1)
    mixed_response = jnp.fft.irfft(fourier_coefficients, n=2 * context_extent, axis=1)[:, :context_extent]
    multiplied_response = (embedded_tokens[0] * (mixed_response + residual_coefficient[:, None] * modulating_sequence)).astype(jnp.bfloat16)
    return jnp.dot(mixer_weight.T, multiplied_response, preferred_element_type=jnp.float32)
```

```python
import functools
import math

import jax
import jax.numpy as jnp
import numpy as np
from jax import lax
from jax.experimental import pallas as pl
from jax.experimental.pallas import tpu as pltpu
from jax.sharding import PartitionSpec as P

HIGHEST = lax.Precision.HIGHEST


def from_behind(shard, axis, by):
    size = lax.axis_size(axis)
    pairs = [(i, i + by) for i in range(size) if 0 <= i + by < size]
    return lax.ppermute(shard, axis, pairs)


def causal_valid(extended, filter_taps, span_out):
    tap_count = filter_taps.shape[0]
    summed = None
    for offset in range(tap_count):
        begin_at = tap_count - 1 - offset
        term = filter_taps[offset][..., None] * extended[..., begin_at : begin_at + span_out]
        summed = term if summed is None else summed + term
    return summed


def square_table(order):
    index = jnp.arange(order, dtype=jnp.int32)
    angle = (index[:, None] * index[None, :] % order).astype(jnp.float32) * (2.0 * math.pi / order)
    return (jnp.cos(angle), jnp.sin(angle))


def make_tables(overall_line_number, adjacent_number):
    first = overall_line_number // 4
    second = 8 * adjacent_number
    padded_len = first * second
    cos_first, sin_first = square_table(first)
    cos_second, sin_second = square_table(second)
    product = (
        jnp.arange(first, dtype=jnp.int32)[:, None] * jnp.arange(second, dtype=jnp.int32)[None, :]
    )
    angle = product.astype(jnp.float32) * (2.0 * math.pi / padded_len)
    return (
        first,
        second,
        padded_len,
        cos_first,
        sin_first,
        cos_second,
        sin_second,
        jnp.cos(angle),
        jnp.sin(angle),
    )


def forward(signal, tables):
    first, second, padded_len, cos_first, sin_first, cos_second, sin_second, twid_cos, twid_sin = (
        tables
    )
    half = first // 2
    blocks = signal.reshape(signal.shape[0], half, second)
    real_one = jnp.einsum("ka,mab->mkb", cos_first[:, :half], blocks, precision=HIGHEST)
    imag_one = -jnp.einsum("ka,mab->mkb", sin_first[:, :half], blocks, precision=HIGHEST)
    real_two = real_one * twid_cos + imag_one * twid_sin
    imag_two = imag_one * twid_cos - real_one * twid_sin
    real_out = jnp.einsum("mkb,bj->mkj", real_two, cos_second, precision=HIGHEST) + jnp.einsum(
        "mkb,bj->mkj", imag_two, sin_second, precision=HIGHEST
    )
    imag_out = jnp.einsum("mkb,bj->mkj", imag_two, cos_second, precision=HIGHEST) - jnp.einsum(
        "mkb,bj->mkj", real_two, sin_second, precision=HIGHEST
    )
    return (real_out, imag_out)


def inverse(spec_real, spec_imag, tables):
    first, second, padded_len, cos_first, sin_first, cos_second, sin_second, twid_cos, twid_sin = (
        tables
    )
    half = first // 2
    real_one = jnp.einsum("mkj,jb->mkb", spec_real, cos_second, precision=HIGHEST) - jnp.einsum(
        "mkj,jb->mkb", spec_imag, sin_second, precision=HIGHEST
    )
    imag_one = jnp.einsum("mkj,jb->mkb", spec_imag, cos_second, precision=HIGHEST) + jnp.einsum(
        "mkj,jb->mkb", spec_real, sin_second, precision=HIGHEST
    )
    real_two = real_one * twid_cos - imag_one * twid_sin
    imag_two = imag_one * twid_cos + real_one * twid_sin
    result = jnp.einsum("ak,mkb->mab", cos_first[:half], real_two, precision=HIGHEST) - jnp.einsum(
        "ak,mkb->mab", sin_first[:half], imag_two, precision=HIGHEST
    )
    return (result / padded_len).reshape(spec_real.shape[0], half * second)


def long_convolve(third_branch_lines, filter_spec, tables):
    val_real, val_imag = forward(third_branch_lines, tables)
    filt_real, filt_imag = filter_spec
    return inverse(
        val_real * filt_real - val_imag * filt_imag,
        val_real * filt_imag + val_imag * filt_real,
        tables,
    )


def shards(
    projected, short_taps, medium_taps, global_kernel_taps, residual_coefficient, mixer_weight
):
    overall_line_number = projected.shape[2]
    chan_local = projected.shape[1]
    adjacent_number = lax.axis_size("seq")
    adjacent_each = chan_local // adjacent_number
    short_span = short_taps.shape[0]
    medium_span = medium_taps.shape[0]
    tables = make_tables(overall_line_number, adjacent_number)
    filter_blocks = global_kernel_taps.reshape(adjacent_number, adjacent_each, overall_line_number)
    short_edge = from_behind(projected[:, :, overall_line_number - (short_span - 1) :], "seq", 1)
    embedded_tokens = causal_valid(
        jnp.concatenate([short_edge, projected], axis=2), short_taps, overall_line_number
    )
    medium_edge = from_behind(
        embedded_tokens[2, :, overall_line_number - (medium_span - 1) :], "seq", 1
    )
    averaged_sequence = causal_valid(
        jnp.concatenate([medium_edge, embedded_tokens[2]], axis=1), medium_taps, overall_line_number
    )
    first_branch_share = embedded_tokens[0]
    second_branch_share = embedded_tokens[1]
    modulating_sequence = second_branch_share * averaged_sequence
    modulating_pieces_array = modulating_sequence.reshape(
        adjacent_number, adjacent_each, overall_line_number
    )
    third_branch_lines = lax.all_to_all(
        modulating_pieces_array, "seq", split_axis=0, concat_axis=2, tiled=True
    )
    filter_piece = lax.all_to_all(filter_blocks, "seq", split_axis=0, concat_axis=2, tiled=True)
    result = long_convolve(third_branch_lines[0], forward(filter_piece[0], tables), tables)
    mixed_response = lax.all_to_all(
        result[None], "seq", split_axis=2, concat_axis=0, tiled=True
    ).reshape(chan_local, overall_line_number)
    multiplied_response = (
        first_branch_share * (mixed_response + residual_coefficient[:, None] * modulating_sequence)
    ).astype(jnp.bfloat16)
    empty = jnp.zeros((mixer_weight.shape[1], overall_line_number), jnp.float32)
    piece = lax.all_gather(multiplied_response, "ch", axis=0, tiled=True)
    weight_rows = lax.slice_in_dim(mixer_weight, 0, piece.shape[0], axis=0)
    return empty + lax.dot_general(
        weight_rows, piece, (((0,), (0,)), ((), ())), preferred_element_type=jnp.float32
    )


LANES = 128
HALO = 136
MESH = pl.DeviceIdType.MESH


def split_np(table):
    high = table.astype(np.float32).astype(jnp.bfloat16)
    low = (table - high.astype(np.float64)).astype(np.float32).astype(jnp.bfloat16)
    return high, low


def spectral_tables(rows):
    span = rows * LANES
    index = np.arange(rows, dtype=np.float64)
    lane = np.arange(LANES, dtype=np.float64)
    first = 2 * np.pi * np.outer(index + 0.25, index) / rows
    twiddle = 2 * np.pi * np.outer(index + 0.25, lane) / span
    second = 2 * np.pi * np.outer(lane, lane) / LANES
    into = np.concatenate([np.cos(first), -np.sin(first)], axis=0)
    high, low = split_np(into)
    into = np.concatenate([high, high, low], axis=1)
    back = np.concatenate([np.cos(first).T, -np.sin(first).T], axis=1) / span
    high, low = split_np(back)
    back = np.concatenate([high, high, low], axis=1)
    cos, sin = np.cos(second), np.sin(second)
    ahead = np.block([[cos, -sin], [sin, cos]])
    ahead = np.stack(split_np(ahead))
    behind = np.block([[cos, sin], [-sin, cos]])
    behind = np.stack(split_np(behind))
    turn = np.stack([np.cos(twiddle), np.sin(twiddle)]).astype(np.float32)
    return into, back, ahead, behind, turn


def split(value):
    high = value.astype(jnp.bfloat16)
    low = (value - high.astype(jnp.float32)).astype(jnp.bfloat16)
    return high, low


def dot(left, right):
    return jnp.dot(left, right, preferred_element_type=jnp.float32)


def dot3(value, table_ref):
    high, low = split(value)
    return dot(high, table_ref[0]) + dot(low, table_ref[0]) + dot(high, table_ref[1])


def to_spectrum(src, spec, each, rows, into_ref, ahead_ref, turn_ref):
    cos, sin = turn_ref[0], turn_ref[1]
    group = 4
    for begin in range(0, each, group):
        lines = [src[pl.ds(begin + i, rows, stride=each), :] for i in range(group)]
        high, low = split(jnp.concatenate(lines, axis=1))
        once = dot(into_ref[...], jnp.concatenate([high, low, high], axis=0))
        turned = []
        for i in range(group):
            real = once[:rows, i * LANES : (i + 1) * LANES]
            imag = once[rows:, i * LANES : (i + 1) * LANES]
            turned.append(
                jnp.concatenate([real * cos + imag * sin, imag * cos - real * sin], axis=1)
            )
        twice = dot3(jnp.concatenate(turned, axis=0), ahead_ref)
        spec[begin * rows : (begin + group) * rows, :] = twice


def from_spectrum(val, filt, dst, each, rows, back_ref, behind_ref, turn_ref):
    cos, sin = turn_ref[0], turn_ref[1]
    group = 4
    for begin in range(0, each, group):
        part = slice(begin * rows, (begin + group) * rows)
        val_real, val_imag = val[part, :LANES], val[part, LANES:]
        filt_real, filt_imag = filt[part, :LANES], filt[part, LANES:]
        product = jnp.concatenate(
            [
                val_real * filt_real - val_imag * filt_imag,
                val_real * filt_imag + val_imag * filt_real,
            ],
            axis=1,
        )
        once = dot3(product, behind_ref)
        turned = []
        for i in range(group):
            real = once[i * rows : (i + 1) * rows, :LANES]
            imag = once[i * rows : (i + 1) * rows, LANES:]
            turned.append(
                jnp.concatenate([real * cos - imag * sin, imag * cos + real * sin], axis=0)
            )
        high, low = split(jnp.concatenate(turned, axis=1))
        lines = dot(back_ref[...], jnp.concatenate([high, low, high], axis=0))
        for i in range(group):
            dst[pl.ds(begin + i, rows, stride=each), :] = lines[:, i * LANES : (i + 1) * LANES]


def kernel(
    seq_size,
    ch_size,
    proj_ref,
    short_ref,
    medium_ref,
    taps_ref,
    resid_ref,
    mix_ref,
    into_ref,
    back_ref,
    ahead_ref,
    behind_ref,
    turn_ref,
    out_ref,
    lines_t,
    feat_v,
    taps_out,
    taps_in,
    carrier,
    carrier_in,
    gate,
    answer,
    answer_in,
    spec_filt,
    spec_val,
    gated,
    halo_send,
    halo_recv,
    taps_send,
    taps_recv,
    carrier_send,
    carrier_recv,
    answer_send,
    answer_recv,
    gated_send,
    gated_recv,
):
    me = lax.axis_index("seq")
    group = lax.axis_index("ch")
    chan, span = proj_ref.shape[1], proj_ref.shape[2]
    short_span = short_ref.shape[0]
    medium_span = medium_ref.shape[0]
    each = chan // seq_size
    blocks = span // LANES
    rows = seq_size * blocks
    slab = blocks * each

    barrier = pltpu.get_barrier_semaphore()
    for step in range(1, seq_size):
        pl.semaphore_signal(
            barrier, 1, device_id={"seq": lax.rem(me + step, seq_size)}, device_id_type=MESH
        )
    for step in range(1, ch_size):
        pl.semaphore_signal(
            barrier, 1, device_id={"ch": lax.rem(group + step, ch_size)}, device_id_type=MESH
        )

    def transpose_in(stream):
        for k in range(blocks):
            lines_t[stream, HALO + k * LANES : HALO + (k + 1) * LANES, :] = proj_ref[
                stream, :, k * LANES : (k + 1) * LANES
            ].T

    def scatter_rows(dst, k, block):
        for s in range(seq_size):
            dst[s * slab + k * each : s * slab + (k + 1) * each, :] = block[
                s * each : (s + 1) * each, :
            ]

    transpose_in(2)
    for k in range(blocks):
        scatter_rows(taps_out, k, taps_ref[:, k * LANES : (k + 1) * LANES])
    transpose_in(1)
    transpose_in(0)
    pl.semaphore_wait(barrier, seq_size - 1 + ch_size - 1)

    def halo_copies():
        after = lax.rem(me + 1, seq_size)
        return [
            pltpu.make_async_remote_copy(
                src_ref=lines_t.at[2, span : span + HALO, :],
                dst_ref=lines_t.at[2, 0:HALO, :],
                send_sem=halo_send.at[0],
                recv_sem=halo_recv.at[0],
                device_id={"seq": after},
                device_id_type=MESH,
            ),
            pltpu.make_async_remote_copy(
                src_ref=lines_t.at[0:2, span + HALO - 8 : span + HALO, :],
                dst_ref=lines_t.at[0:2, HALO - 8 : HALO, :],
                send_sem=halo_send.at[1],
                recv_sem=halo_recv.at[1],
                device_id={"seq": after},
                device_id_type=MESH,
            ),
        ]

    @pl.when(me < seq_size - 1)
    def _():
        for copy in halo_copies():
            copy.start()

    def exchange(src, dst, send, recv):
        copies = []
        for step in range(1, seq_size):
            peer = lax.rem(me + step, seq_size)
            copies.append(
                pltpu.make_async_remote_copy(
                    src_ref=src.at[pl.ds(pl.multiple_of(peer * slab, 8), slab), :],
                    dst_ref=dst.at[pl.ds(pl.multiple_of(me * slab, 8), slab), :],
                    send_sem=send.at[step],
                    recv_sem=recv.at[step],
                    device_id={"seq": peer},
                    device_id_type=MESH,
                )
            )
        for copy in copies:
            copy.start()
        own = pl.ds(pl.multiple_of(me * slab, 8), slab)
        dst[own, :] = src[own, :]
        return copies

    taps_copies = exchange(taps_out, taps_in, taps_send, taps_recv)

    @pl.when(me == 0)
    def _():
        lines_t[2, 0:HALO, :] = jnp.zeros((HALO, chan), jnp.float32)
        lines_t[0:2, HALO - 8 : HALO, :] = jnp.zeros((2, 8, chan), jnp.float32)

    @pl.when(me > 0)
    def _():
        for copy in halo_copies():
            copy.wait_recv()

    def short(stream, begin, count):
        total = None
        for j in range(short_span):
            term = (
                short_ref[j, stream : stream + 1, :]
                * lines_t[stream, begin - j : begin - j + count, :]
            )
            total = term if total is None else total + term
        return total

    for begin in range(0, LANES + span, LANES):
        feat_v[begin : begin + LANES, :] = short(2, HALO - LANES + begin, LANES)

    tile = 8

    for k in range(blocks):
        base = (k + 1) * LANES

        def taps_body(m, total):
            for r in range(tile):
                j = m * tile + r
                start = base - r - m * tile
                total = total + medium_ref[pl.ds(j, 1), :] * feat_v[pl.ds(start, LANES), :]
            return total

        smooth = lax.fori_loop(
            0, medium_span // tile, taps_body, jnp.zeros((LANES, chan), jnp.float32)
        )
        block = short(1, HALO + k * LANES, LANES) * smooth
        scatter_rows(carrier, k, block.T)

    carrier_copies = exchange(carrier, carrier_in, carrier_send, carrier_recv)

    for copy in taps_copies:
        copy.wait_recv()
    to_spectrum(taps_in, spec_filt, each, rows, into_ref, ahead_ref, turn_ref)
    for k in range(blocks):
        scatter_rows(gate, k, short(0, HALO + k * LANES, LANES).T)
    resid = jnp.broadcast_to(resid_ref[...], (LANES, chan)).T

    for copy in carrier_copies:
        copy.wait_recv()
    to_spectrum(carrier_in, spec_val, each, rows, into_ref, ahead_ref, turn_ref)
    from_spectrum(spec_val, spec_filt, answer, each, rows, back_ref, behind_ref, turn_ref)
    answer_copies = exchange(answer, answer_in, answer_send, answer_recv)
    for copy in answer_copies:
        copy.wait_recv()

    for s in range(seq_size):
        weight = resid[s * each : (s + 1) * each, :]
        for k in range(blocks):
            part = slice(s * slab + k * each, s * slab + (k + 1) * each)
            value = gate[part, :] * (answer_in[part, :] + weight * carrier[part, :])
            gated[group, s * each : (s + 1) * each, k * LANES : (k + 1) * LANES] = value.astype(
                jnp.bfloat16
            )

    gated_copies = []
    for step in range(1, ch_size):
        copy = pltpu.make_async_remote_copy(
            src_ref=gated.at[group],
            dst_ref=gated.at[group],
            send_sem=gated_send.at[step],
            recv_sem=gated_recv.at[step],
            device_id={"ch": lax.rem(group + step, ch_size)},
            device_id_type=MESH,
        )
        copy.start()
        gated_copies.append(copy)

    def mixed(owner):
        weight = mix_ref[pl.ds(pl.multiple_of(owner * chan, LANES), chan), :]
        return lax.dot_general(
            weight, gated[owner], (((0,), (0,)), ((), ())), preferred_element_type=jnp.float32
        )

    total = mixed(group)
    for step in range(1, ch_size):
        gated_copies[step - 1].wait_recv()
        total = total + mixed(lax.rem(group - step + ch_size, ch_size))
    out_ref[...] = total

    @pl.when(me < seq_size - 1)
    def _():
        for copy in halo_copies():
            copy.wait_send()

    for copy in taps_copies + carrier_copies + answer_copies + gated_copies:
        copy.wait_send()


def fused(
    projected, short_taps, medium_taps, global_kernel_taps, residual_coefficient, mixer_weight
):
    seq_size, ch_size = lax.axis_size("seq"), lax.axis_size("ch")
    chan, span = projected.shape[1], projected.shape[2]
    each = chan // seq_size
    rows = seq_size * span // LANES
    tables = [jnp.asarray(table) for table in spectral_tables(rows)]
    vmem = pl.BlockSpec(memory_space=pltpu.VMEM)
    plane = pltpu.VMEM((chan * span // LANES, LANES), jnp.float32)
    spectrum = pltpu.VMEM((each * rows, 2 * LANES), jnp.float32)
    dma = pltpu.SemaphoreType.DMA
    return pl.pallas_call(
        functools.partial(kernel, seq_size, ch_size),
        out_shape=jax.ShapeDtypeStruct((mixer_weight.shape[1], span), jnp.float32),
        in_specs=[vmem] * 11,
        out_specs=vmem,
        scratch_shapes=[
            pltpu.VMEM((3, HALO + span, chan), jnp.float32),
            pltpu.VMEM((LANES + span, chan), jnp.float32),
            plane,
            plane,
            plane,
            plane,
            plane,
            plane,
            plane,
            spectrum,
            spectrum,
            pltpu.VMEM((ch_size, chan, span), jnp.bfloat16),
            dma((2,)),
            dma((2,)),
            dma((seq_size,)),
            dma((seq_size,)),
            dma((seq_size,)),
            dma((seq_size,)),
            dma((seq_size,)),
            dma((seq_size,)),
            dma((ch_size,)),
            dma((ch_size,)),
        ],
        compiler_params=pltpu.CompilerParams(
            collective_id=0, has_side_effects=True, vmem_limit_bytes=40 * 2**20
        ),
        name="hyena",
    )(
        projected,
        short_taps,
        medium_taps,
        global_kernel_taps,
        residual_coefficient.reshape(1, chan),
        mixer_weight,
        *tables,
    )


def block(
    projected, short_taps, medium_taps, global_kernel_taps, residual_coefficient, mixer_weight
):
    operands = (
        projected,
        short_taps,
        medium_taps,
        global_kernel_taps,
        residual_coefficient,
        mixer_weight,
    )
    chan, span = projected.shape[1], projected.shape[2]
    each = chan // lax.axis_size("seq")
    fits = (
        chan == LANES
        and span % LANES == 0
        and span >= HALO
        and each % 16 == 0
        and medium_taps.shape[0] == LANES
        and short_taps.shape[0] <= 8
        and chan * span * 4 <= 2**20
    )
    return fused(*operands) if fits else shards(*operands)


def solution(mesh):
    return jax.shard_map(
        block,
        mesh=mesh,
        in_specs=(
            P(None, "ch", "seq"),
            P(None, None, "ch"),
            P(None, "ch"),
            P("ch", "seq"),
            P("ch"),
            P(None, "ch"),
        ),
        out_specs=P("ch", "seq"),
        check_vma=False,
    )
```

```python
import functools
import math

import jax
import jax.numpy as jnp
import numpy as np
from jax import lax
from jax.experimental import pallas as pl
from jax.experimental.pallas import tpu as pltpu
from jax.sharding import PartitionSpec as P

HIGHEST = lax.Precision.HIGHEST


def from_behind(shard, axis, by):
    size = lax.axis_size(axis)
    pairs = [(i, i + by) for i in range(size) if 0 <= i + by < size]
    return lax.ppermute(shard, axis, pairs)


def causal_valid(extended, filter_taps, span_out):
    tap_count = filter_taps.shape[0]
    summed = None
    for offset in range(tap_count):
        begin_at = tap_count - 1 - offset
        term = filter_taps[offset][..., None] * extended[..., begin_at : begin_at + span_out]
        summed = term if summed is None else summed + term
    return summed


def square_table(order):
    index = jnp.arange(order, dtype=jnp.int32)
    angle = (index[:, None] * index[None, :] % order).astype(jnp.float32) * (2.0 * math.pi / order)
    return (jnp.cos(angle), jnp.sin(angle))


def make_tables(overall_line_number, adjacent_number):
    first = overall_line_number // 4
    second = 8 * adjacent_number
    padded_len = first * second
    cos_first, sin_first = square_table(first)
    cos_second, sin_second = square_table(second)
    product = (
        jnp.arange(first, dtype=jnp.int32)[:, None] * jnp.arange(second, dtype=jnp.int32)[None, :]
    )
    angle = product.astype(jnp.float32) * (2.0 * math.pi / padded_len)
    return (
        first,
        second,
        padded_len,
        cos_first,
        sin_first,
        cos_second,
        sin_second,
        jnp.cos(angle),
        jnp.sin(angle),
    )


def forward(signal, tables):
    first, second, padded_len, cos_first, sin_first, cos_second, sin_second, twid_cos, twid_sin = (
        tables
    )
    half = first // 2
    blocks = signal.reshape(signal.shape[0], half, second)
    real_one = jnp.einsum("ka,mab->mkb", cos_first[:, :half], blocks, precision=HIGHEST)
    imag_one = -jnp.einsum("ka,mab->mkb", sin_first[:, :half], blocks, precision=HIGHEST)
    real_two = real_one * twid_cos + imag_one * twid_sin
    imag_two = imag_one * twid_cos - real_one * twid_sin
    real_out = jnp.einsum("mkb,bj->mkj", real_two, cos_second, precision=HIGHEST) + jnp.einsum(
        "mkb,bj->mkj", imag_two, sin_second, precision=HIGHEST
    )
    imag_out = jnp.einsum("mkb,bj->mkj", imag_two, cos_second, precision=HIGHEST) - jnp.einsum(
        "mkb,bj->mkj", real_two, sin_second, precision=HIGHEST
    )
    return (real_out, imag_out)


def inverse(spec_real, spec_imag, tables):
    first, second, padded_len, cos_first, sin_first, cos_second, sin_second, twid_cos, twid_sin = (
        tables
    )
    half = first // 2
    real_one = jnp.einsum("mkj,jb->mkb", spec_real, cos_second, precision=HIGHEST) - jnp.einsum(
        "mkj,jb->mkb", spec_imag, sin_second, precision=HIGHEST
    )
    imag_one = jnp.einsum("mkj,jb->mkb", spec_imag, cos_second, precision=HIGHEST) + jnp.einsum(
        "mkj,jb->mkb", spec_real, sin_second, precision=HIGHEST
    )
    real_two = real_one * twid_cos - imag_one * twid_sin
    imag_two = imag_one * twid_cos + real_one * twid_sin
    result = jnp.einsum("ak,mkb->mab", cos_first[:half], real_two, precision=HIGHEST) - jnp.einsum(
        "ak,mkb->mab", sin_first[:half], imag_two, precision=HIGHEST
    )
    return (result / padded_len).reshape(spec_real.shape[0], half * second)


def long_convolve(third_branch_lines, filter_spec, tables):
    val_real, val_imag = forward(third_branch_lines, tables)
    filt_real, filt_imag = filter_spec
    return inverse(
        val_real * filt_real - val_imag * filt_imag,
        val_real * filt_imag + val_imag * filt_real,
        tables,
    )


def shards(
    projected, short_taps, medium_taps, global_kernel_taps, residual_coefficient, mixer_weight
):
    overall_line_number = projected.shape[2]
    chan_local = projected.shape[1]
    adjacent_number = lax.axis_size("seq")
    adjacent_each = chan_local // adjacent_number
    short_span = short_taps.shape[0]
    medium_span = medium_taps.shape[0]
    tables = make_tables(overall_line_number, adjacent_number)
    filter_blocks = global_kernel_taps.reshape(adjacent_number, adjacent_each, overall_line_number)
    short_edge = from_behind(projected[:, :, overall_line_number - (short_span - 1) :], "seq", 1)
    embedded_tokens = causal_valid(
        jnp.concatenate([short_edge, projected], axis=2), short_taps, overall_line_number
    )
    medium_edge = from_behind(
        embedded_tokens[2, :, overall_line_number - (medium_span - 1) :], "seq", 1
    )
    averaged_sequence = causal_valid(
        jnp.concatenate([medium_edge, embedded_tokens[2]], axis=1), medium_taps, overall_line_number
    )
    first_branch_share = embedded_tokens[0]
    second_branch_share = embedded_tokens[1]
    modulating_sequence = second_branch_share * averaged_sequence
    modulating_pieces_array = modulating_sequence.reshape(
        adjacent_number, adjacent_each, overall_line_number
    )
    third_branch_lines = lax.all_to_all(
        modulating_pieces_array, "seq", split_axis=0, concat_axis=2, tiled=True
    )
    filter_piece = lax.all_to_all(filter_blocks, "seq", split_axis=0, concat_axis=2, tiled=True)
    result = long_convolve(third_branch_lines[0], forward(filter_piece[0], tables), tables)
    mixed_response = lax.all_to_all(
        result[None], "seq", split_axis=2, concat_axis=0, tiled=True
    ).reshape(chan_local, overall_line_number)
    multiplied_response = (
        first_branch_share * (mixed_response + residual_coefficient[:, None] * modulating_sequence)
    ).astype(jnp.bfloat16)
    empty = jnp.zeros((mixer_weight.shape[1], overall_line_number), jnp.float32)
    piece = lax.all_gather(multiplied_response, "ch", axis=0, tiled=True)
    weight_rows = lax.slice_in_dim(mixer_weight, 0, piece.shape[0], axis=0)
    return empty + lax.dot_general(
        weight_rows, piece, (((0,), (0,)), ((), ())), preferred_element_type=jnp.float32
    )


LANES = 128
HALO = 136
PARTS = 2
MESH = pl.DeviceIdType.MESH


def split_np(table):
    high = table.astype(np.float32).astype(jnp.bfloat16)
    low = (table - high.astype(np.float64)).astype(np.float32).astype(jnp.bfloat16)
    return high, low


def spectral_tables(rows):
    span = rows * LANES
    index = np.arange(rows, dtype=np.float64)
    lane = np.arange(LANES, dtype=np.float64)
    first = 2 * np.pi * np.outer(index + 0.25, index) / rows
    twiddle = 2 * np.pi * np.outer(index + 0.25, lane) / span
    second = 2 * np.pi * np.outer(lane, lane) / LANES
    into = np.concatenate([np.cos(first), -np.sin(first)], axis=0)
    high, low = split_np(into)
    into = np.concatenate([high, high, low], axis=1)
    back = np.concatenate([np.cos(first).T, -np.sin(first).T], axis=1) / span
    high, low = split_np(back)
    back = np.concatenate([high, high, low], axis=1)
    cos, sin = np.cos(second), np.sin(second)
    ahead = np.block([[cos, -sin], [sin, cos]])
    ahead = np.stack(split_np(ahead))
    behind = np.block([[cos, sin], [-sin, cos]])
    behind = np.stack(split_np(behind))
    turn = np.stack([np.cos(twiddle), np.sin(twiddle)]).astype(np.float32)
    return into, back, ahead, behind, turn


def split(value):
    high = value.astype(jnp.bfloat16)
    low = (value - high.astype(jnp.float32)).astype(jnp.bfloat16)
    return high, low


def dot(left, right):
    return jnp.dot(left, right, preferred_element_type=jnp.float32)


def dot3(value, table_ref):
    high, low = split(value)
    return dot(high, table_ref[0]) + dot(low, table_ref[0]) + dot(high, table_ref[1])


def to_spectrum(src, spec, each, rows, into_ref, ahead_ref, turn_ref):
    cos, sin = turn_ref[0], turn_ref[1]
    group = 4
    for begin in range(0, each, group):
        lines = [src[pl.ds(begin + i, rows, stride=each), :] for i in range(group)]
        high, low = split(jnp.concatenate(lines, axis=1))
        once = dot(into_ref[...], jnp.concatenate([high, low, high], axis=0))
        turned = []
        for i in range(group):
            real = once[:rows, i * LANES : (i + 1) * LANES]
            imag = once[rows:, i * LANES : (i + 1) * LANES]
            turned.append(
                jnp.concatenate([real * cos + imag * sin, imag * cos - real * sin], axis=1)
            )
        twice = dot3(jnp.concatenate(turned, axis=0), ahead_ref)
        spec[begin * rows : (begin + group) * rows, :] = twice


def from_spectrum(val, filt, dst, each, rows, back_ref, behind_ref, turn_ref):
    cos, sin = turn_ref[0], turn_ref[1]
    group = 4
    for begin in range(0, each, group):
        part = slice(begin * rows, (begin + group) * rows)
        val_real, val_imag = val[part, :LANES], val[part, LANES:]
        filt_real, filt_imag = filt[part, :LANES], filt[part, LANES:]
        product = jnp.concatenate(
            [
                val_real * filt_real - val_imag * filt_imag,
                val_real * filt_imag + val_imag * filt_real,
            ],
            axis=1,
        )
        once = dot3(product, behind_ref)
        turned = []
        for i in range(group):
            real = once[i * rows : (i + 1) * rows, :LANES]
            imag = once[i * rows : (i + 1) * rows, LANES:]
            turned.append(
                jnp.concatenate([real * cos - imag * sin, imag * cos + real * sin], axis=0)
            )
        high, low = split(jnp.concatenate(turned, axis=1))
        lines = dot(back_ref[...], jnp.concatenate([high, low, high], axis=0))
        for i in range(group):
            dst[pl.ds(begin + i, rows, stride=each), :] = lines[:, i * LANES : (i + 1) * LANES]


def kernel(
    seq_size,
    ch_size,
    proj_hbm,
    short_hbm,
    medium_hbm,
    taps_hbm,
    resid_hbm,
    mix_hbm,
    into_hbm,
    back_hbm,
    ahead_hbm,
    behind_hbm,
    turn_hbm,
    out_ref,
    proj_ref,
    short_ref,
    medium_ref,
    taps_ref,
    resid_ref,
    mix_ref,
    into_ref,
    back_ref,
    ahead_ref,
    behind_ref,
    turn_ref,
    stage_sem,
    proj_sem,
    lines_t,
    feat_v,
    taps_out,
    taps_in,
    carrier,
    carrier_in,
    gate,
    answer,
    answer_in,
    spec_filt,
    spec_val,
    gated,
    halo_send,
    halo_recv,
    taps_send,
    taps_recv,
    carrier_send,
    carrier_recv,
    answer_send,
    answer_recv,
    gated_send,
    gated_recv,
):
    me = lax.axis_index("seq")
    group = lax.axis_index("ch")
    chan, span = proj_ref.shape[1], proj_ref.shape[2]
    short_span = short_ref.shape[1]
    medium_span = medium_ref.shape[0]
    each = chan // seq_size // PARTS
    blocks = span // LANES
    rows = seq_size * blocks
    slab = blocks * each
    part_chan = chan // PARTS

    proj_copies = {
        stream: pltpu.make_async_copy(
            proj_hbm.at[stream], proj_ref.at[stream], proj_sem.at[stream]
        )
        for stream in (2, 1, 0)
    }
    staged = {}
    for i, (name, src, dst) in enumerate(
        (
            ("taps", taps_hbm, taps_ref),
            ("short", short_hbm, short_ref),
            ("medium", medium_hbm, medium_ref),
            ("into", into_hbm, into_ref),
            ("turn", turn_hbm, turn_ref),
            ("ahead", ahead_hbm, ahead_ref),
            ("behind", behind_hbm, behind_ref),
            ("back", back_hbm, back_ref),
            ("resid", resid_hbm, resid_ref),
            ("mix", mix_hbm, mix_ref),
        )
    ):
        staged[name] = pltpu.make_async_copy(src, dst, stage_sem.at[i])
    proj_copies[2].start()
    staged["taps"].start()
    proj_copies[1].start()
    proj_copies[0].start()
    for name in staged:
        if name != "taps":
            staged[name].start()

    barrier = pltpu.get_barrier_semaphore()
    for step in range(1, seq_size):
        pl.semaphore_signal(
            barrier, 1, device_id={"seq": lax.rem(me + step, seq_size)}, device_id_type=MESH
        )
    for step in range(1, ch_size):
        pl.semaphore_signal(
            barrier, 1, device_id={"ch": lax.rem(group + step, ch_size)}, device_id_type=MESH
        )

    def transpose_in(stream):
        for k in range(blocks):
            lines_t[stream, HALO + k * LANES : HALO + (k + 1) * LANES, :] = proj_ref[
                stream, :, k * LANES : (k + 1) * LANES
            ].T

    def scatter_rows(dst, k, block):
        for part in range(PARTS):
            for s in range(seq_size):
                begin = s * slab + k * each
                first = part * part_chan + s * each
                dst[part, begin : begin + each, :] = block[first : first + each, :]

    proj_copies[2].wait()
    transpose_in(2)
    staged["taps"].wait()
    for k in range(blocks):
        scatter_rows(taps_out, k, taps_ref[:, k * LANES : (k + 1) * LANES])
    proj_copies[1].wait()
    transpose_in(1)
    proj_copies[0].wait()
    transpose_in(0)
    pl.semaphore_wait(barrier, seq_size - 1 + ch_size - 1)

    def halo_copies():
        after = lax.rem(me + 1, seq_size)
        return [
            pltpu.make_async_remote_copy(
                src_ref=lines_t.at[2, span : span + HALO, :],
                dst_ref=lines_t.at[2, 0:HALO, :],
                send_sem=halo_send.at[0],
                recv_sem=halo_recv.at[0],
                device_id={"seq": after},
                device_id_type=MESH,
            ),
            pltpu.make_async_remote_copy(
                src_ref=lines_t.at[0:2, span + HALO - 8 : span + HALO, :],
                dst_ref=lines_t.at[0:2, HALO - 8 : HALO, :],
                send_sem=halo_send.at[1],
                recv_sem=halo_recv.at[1],
                device_id={"seq": after},
                device_id_type=MESH,
            ),
        ]

    @pl.when(me < seq_size - 1)
    def _():
        for copy in halo_copies():
            copy.start()

    def exchange(src, dst, send, recv, part):
        src, dst, send, recv = src.at[part], dst.at[part], send.at[part], recv.at[part]
        copies = []
        for step in range(1, seq_size):
            peer = lax.rem(me + step, seq_size)
            copies.append(
                pltpu.make_async_remote_copy(
                    src_ref=src.at[pl.ds(pl.multiple_of(peer * slab, 8), slab), :],
                    dst_ref=dst.at[pl.ds(pl.multiple_of(me * slab, 8), slab), :],
                    send_sem=send.at[step],
                    recv_sem=recv.at[step],
                    device_id={"seq": peer},
                    device_id_type=MESH,
                )
            )
        for copy in copies:
            copy.start()
        own = pl.ds(pl.multiple_of(me * slab, 8), slab)
        dst[own, :] = src[own, :]
        return copies

    every = range(PARTS)
    taps_copies = [exchange(taps_out, taps_in, taps_send, taps_recv, part) for part in every]
    staged["short"].wait()
    staged["medium"].wait()

    @pl.when(me == 0)
    def _():
        lines_t[2, 0:HALO, :] = jnp.zeros((HALO, chan), jnp.float32)
        lines_t[0:2, HALO - 8 : HALO, :] = jnp.zeros((2, 8, chan), jnp.float32)

    @pl.when(me > 0)
    def _():
        for copy in halo_copies():
            copy.wait_recv()

    def short(stream, begin, count):
        total = None
        for j in range(short_span):
            term = (
                short_ref[stream, j : j + 1, :]
                * lines_t[stream, begin - j : begin - j + count, :]
            )
            total = term if total is None else total + term
        return total

    for begin in range(0, LANES + span, LANES):
        feat_v[begin : begin + LANES, :] = short(2, HALO - LANES + begin, LANES)

    tile = 8

    for k in range(blocks):
        base = (k + 1) * LANES

        def taps_body(m, total):
            for r in range(tile):
                j = m * tile + r
                start = base - r - m * tile
                total = total + medium_ref[pl.ds(j, 1), :] * feat_v[pl.ds(start, LANES), :]
            return total

        smooth = lax.fori_loop(
            0, medium_span // tile, taps_body, jnp.zeros((LANES, chan), jnp.float32)
        )
        block = short(1, HALO + k * LANES, LANES) * smooth
        scatter_rows(carrier, k, block.T)

    carrier_copies = [
        exchange(carrier, carrier_in, carrier_send, carrier_recv, part) for part in every
    ]

    for name in ("into", "turn", "ahead", "behind", "back", "resid", "mix"):
        staged[name].wait()
    for part in every:
        for copy in taps_copies[part]:
            copy.wait_recv()
        to_spectrum(
            taps_in.at[part], spec_filt.at[part], each, rows, into_ref, ahead_ref, turn_ref
        )
    for k in range(blocks):
        scatter_rows(gate, k, short(0, HALO + k * LANES, LANES).T)
    resid = jnp.broadcast_to(resid_ref[...], (LANES, chan)).T

    answer_copies = []
    for part in every:
        for copy in carrier_copies[part]:
            copy.wait_recv()
        to_spectrum(carrier_in.at[part], spec_val, each, rows, into_ref, ahead_ref, turn_ref)
        from_spectrum(
            spec_val,
            spec_filt.at[part],
            answer.at[part],
            each,
            rows,
            back_ref,
            behind_ref,
            turn_ref,
        )
        answer_copies.append(exchange(answer, answer_in, answer_send, answer_recv, part))

    gated_copies = []
    for part in every:
        for copy in answer_copies[part]:
            copy.wait_recv()
        for s in range(seq_size):
            first = part * part_chan + s * each
            weight = resid[first : first + each, :]
            for k in range(blocks):
                piece = slice(s * slab + k * each, s * slab + (k + 1) * each)
                value = gate[part, piece, :] * (
                    answer_in[part, piece, :] + weight * carrier[part, piece, :]
                )
                gated[group, first : first + each, k * LANES : (k + 1) * LANES] = value.astype(
                    jnp.bfloat16
                )
        lines = slice(part * part_chan, (part + 1) * part_chan)
        for step in range(1, ch_size):
            copy = pltpu.make_async_remote_copy(
                src_ref=gated.at[group, lines, :],
                dst_ref=gated.at[group, lines, :],
                send_sem=gated_send.at[part, step],
                recv_sem=gated_recv.at[part, step],
                device_id={"ch": lax.rem(group + step, ch_size)},
                device_id_type=MESH,
            )
            copy.start()
            gated_copies.append((step, copy))

    def mixed(owner):
        weight = mix_ref[pl.ds(pl.multiple_of(owner * chan, LANES), chan), :]
        return lax.dot_general(
            weight, gated[owner], (((0,), (0,)), ((), ())), preferred_element_type=jnp.float32
        )

    total = mixed(group)
    for step in range(1, ch_size):
        for owner_step, copy in gated_copies:
            if owner_step == step:
                copy.wait_recv()
        total = total + mixed(lax.rem(group - step + ch_size, ch_size))
    out_ref[...] = total

    @pl.when(me < seq_size - 1)
    def _():
        for copy in halo_copies():
            copy.wait_send()

    for copies in taps_copies + carrier_copies + answer_copies:
        for copy in copies:
            copy.wait_send()
    for _, copy in gated_copies:
        copy.wait_send()


def fused(
    projected, short_taps, medium_taps, global_kernel_taps, residual_coefficient, mixer_weight
):
    seq_size, ch_size = lax.axis_size("seq"), lax.axis_size("ch")
    chan, span = projected.shape[1], projected.shape[2]
    each = chan // seq_size
    rows = seq_size * span // LANES
    tables = [jnp.asarray(table) for table in spectral_tables(rows)]
    vmem = pl.BlockSpec(memory_space=pltpu.VMEM)
    plane = pltpu.VMEM((PARTS, chan * span // LANES // PARTS, LANES), jnp.float32)
    spectrum = (each // PARTS * rows, 2 * LANES)
    dma = pltpu.SemaphoreType.DMA
    operands = (
        projected,
        short_taps.transpose(1, 0, 2),
        medium_taps,
        global_kernel_taps,
        residual_coefficient.reshape(1, chan),
        mixer_weight,
        *tables,
    )
    return pl.pallas_call(
        functools.partial(kernel, seq_size, ch_size),
        out_shape=jax.ShapeDtypeStruct((mixer_weight.shape[1], span), jnp.float32),
        in_specs=[pl.BlockSpec(memory_space=pl.ANY)] * len(operands),
        out_specs=vmem,
        scratch_shapes=[pltpu.VMEM(x.shape, x.dtype) for x in operands]
        + [
            dma((10,)),
            dma((3,)),
            pltpu.VMEM((3, HALO + span, chan), jnp.float32),
            pltpu.VMEM((LANES + span, chan), jnp.float32),
            plane,
            plane,
            plane,
            plane,
            plane,
            plane,
            plane,
            pltpu.VMEM((PARTS, *spectrum), jnp.float32),
            pltpu.VMEM(spectrum, jnp.float32),
            pltpu.VMEM((ch_size, chan, span), jnp.bfloat16),
            dma((2,)),
            dma((2,)),
            dma((PARTS, seq_size)),
            dma((PARTS, seq_size)),
            dma((PARTS, seq_size)),
            dma((PARTS, seq_size)),
            dma((PARTS, seq_size)),
            dma((PARTS, seq_size)),
            dma((PARTS, ch_size)),
            dma((PARTS, ch_size)),
        ],
        compiler_params=pltpu.CompilerParams(
            collective_id=0, has_side_effects=True, vmem_limit_bytes=60 * 2**20
        ),
        name="hyena",
    )(*operands)


def block(
    projected, short_taps, medium_taps, global_kernel_taps, residual_coefficient, mixer_weight
):
    operands = (
        projected,
        short_taps,
        medium_taps,
        global_kernel_taps,
        residual_coefficient,
        mixer_weight,
    )
    chan, span = projected.shape[1], projected.shape[2]
    each = chan // lax.axis_size("seq")
    fits = (
        chan == LANES
        and span % LANES == 0
        and span >= HALO
        and each % 16 == 0
        and medium_taps.shape[0] == LANES
        and short_taps.shape[0] <= 8
        and chan * span * 4 <= 2**20
    )
    return fused(*operands) if fits else shards(*operands)


def solution(mesh):
    return jax.shard_map(
        block,
        mesh=mesh,
        in_specs=(
            P(None, "ch", "seq"),
            P(None, None, "ch"),
            P(None, "ch"),
            P("ch", "seq"),
            P("ch"),
            P(None, "ch"),
        ),
        out_specs=P("ch", "seq"),
        check_vma=False,
    )
```

```python
import functools
import math

import jax
import jax.numpy as jnp
import numpy as np
from jax import lax
from jax.experimental import pallas as pl
from jax.experimental.pallas import tpu as pltpu
from jax.sharding import PartitionSpec as P

HIGHEST = lax.Precision.HIGHEST


def from_behind(shard, axis, by):
    size = lax.axis_size(axis)
    pairs = [(i, i + by) for i in range(size) if 0 <= i + by < size]
    return lax.ppermute(shard, axis, pairs)


def causal_valid(extended, filter_taps, span_out):
    tap_count = filter_taps.shape[0]
    summed = None
    for offset in range(tap_count):
        begin_at = tap_count - 1 - offset
        term = filter_taps[offset][..., None] * extended[..., begin_at : begin_at + span_out]
        summed = term if summed is None else summed + term
    return summed


def square_table(order):
    index = jnp.arange(order, dtype=jnp.int32)
    angle = (index[:, None] * index[None, :] % order).astype(jnp.float32) * (2.0 * math.pi / order)
    return (jnp.cos(angle), jnp.sin(angle))


def make_tables(overall_line_number, adjacent_number):
    first = overall_line_number // 4
    second = 8 * adjacent_number
    padded_len = first * second
    cos_first, sin_first = square_table(first)
    cos_second, sin_second = square_table(second)
    product = (
        jnp.arange(first, dtype=jnp.int32)[:, None] * jnp.arange(second, dtype=jnp.int32)[None, :]
    )
    angle = product.astype(jnp.float32) * (2.0 * math.pi / padded_len)
    return (
        first,
        second,
        padded_len,
        cos_first,
        sin_first,
        cos_second,
        sin_second,
        jnp.cos(angle),
        jnp.sin(angle),
    )


def forward(signal, tables):
    first, second, padded_len, cos_first, sin_first, cos_second, sin_second, twid_cos, twid_sin = (
        tables
    )
    half = first // 2
    blocks = signal.reshape(signal.shape[0], half, second)
    real_one = jnp.einsum("ka,mab->mkb", cos_first[:, :half], blocks, precision=HIGHEST)
    imag_one = -jnp.einsum("ka,mab->mkb", sin_first[:, :half], blocks, precision=HIGHEST)
    real_two = real_one * twid_cos + imag_one * twid_sin
    imag_two = imag_one * twid_cos - real_one * twid_sin
    real_out = jnp.einsum("mkb,bj->mkj", real_two, cos_second, precision=HIGHEST) + jnp.einsum(
        "mkb,bj->mkj", imag_two, sin_second, precision=HIGHEST
    )
    imag_out = jnp.einsum("mkb,bj->mkj", imag_two, cos_second, precision=HIGHEST) - jnp.einsum(
        "mkb,bj->mkj", real_two, sin_second, precision=HIGHEST
    )
    return (real_out, imag_out)


def inverse(spec_real, spec_imag, tables):
    first, second, padded_len, cos_first, sin_first, cos_second, sin_second, twid_cos, twid_sin = (
        tables
    )
    half = first // 2
    real_one = jnp.einsum("mkj,jb->mkb", spec_real, cos_second, precision=HIGHEST) - jnp.einsum(
        "mkj,jb->mkb", spec_imag, sin_second, precision=HIGHEST
    )
    imag_one = jnp.einsum("mkj,jb->mkb", spec_imag, cos_second, precision=HIGHEST) + jnp.einsum(
        "mkj,jb->mkb", spec_real, sin_second, precision=HIGHEST
    )
    real_two = real_one * twid_cos - imag_one * twid_sin
    imag_two = imag_one * twid_cos + real_one * twid_sin
    result = jnp.einsum("ak,mkb->mab", cos_first[:half], real_two, precision=HIGHEST) - jnp.einsum(
        "ak,mkb->mab", sin_first[:half], imag_two, precision=HIGHEST
    )
    return (result / padded_len).reshape(spec_real.shape[0], half * second)


def long_convolve(third_branch_lines, filter_spec, tables):
    val_real, val_imag = forward(third_branch_lines, tables)
    filt_real, filt_imag = filter_spec
    return inverse(
        val_real * filt_real - val_imag * filt_imag,
        val_real * filt_imag + val_imag * filt_real,
        tables,
    )


def shards(
    projected, short_taps, medium_taps, global_kernel_taps, residual_coefficient, mixer_weight
):
    overall_line_number = projected.shape[2]
    chan_local = projected.shape[1]
    adjacent_number = lax.axis_size("seq")
    adjacent_each = chan_local // adjacent_number
    short_span = short_taps.shape[0]
    medium_span = medium_taps.shape[0]
    tables = make_tables(overall_line_number, adjacent_number)
    filter_blocks = global_kernel_taps.reshape(adjacent_number, adjacent_each, overall_line_number)
    short_edge = from_behind(projected[:, :, overall_line_number - (short_span - 1) :], "seq", 1)
    embedded_tokens = causal_valid(
        jnp.concatenate([short_edge, projected], axis=2), short_taps, overall_line_number
    )
    medium_edge = from_behind(
        embedded_tokens[2, :, overall_line_number - (medium_span - 1) :], "seq", 1
    )
    averaged_sequence = causal_valid(
        jnp.concatenate([medium_edge, embedded_tokens[2]], axis=1), medium_taps, overall_line_number
    )
    first_branch_share = embedded_tokens[0]
    second_branch_share = embedded_tokens[1]
    modulating_sequence = second_branch_share * averaged_sequence
    modulating_pieces_array = modulating_sequence.reshape(
        adjacent_number, adjacent_each, overall_line_number
    )
    third_branch_lines = lax.all_to_all(
        modulating_pieces_array, "seq", split_axis=0, concat_axis=2, tiled=True
    )
    filter_piece = lax.all_to_all(filter_blocks, "seq", split_axis=0, concat_axis=2, tiled=True)
    result = long_convolve(third_branch_lines[0], forward(filter_piece[0], tables), tables)
    mixed_response = lax.all_to_all(
        result[None], "seq", split_axis=2, concat_axis=0, tiled=True
    ).reshape(chan_local, overall_line_number)
    multiplied_response = (
        first_branch_share * (mixed_response + residual_coefficient[:, None] * modulating_sequence)
    ).astype(jnp.bfloat16)
    empty = jnp.zeros((mixer_weight.shape[1], overall_line_number), jnp.float32)
    piece = lax.all_gather(multiplied_response, "ch", axis=0, tiled=True)
    weight_rows = lax.slice_in_dim(mixer_weight, 0, piece.shape[0], axis=0)
    return empty + lax.dot_general(
        weight_rows, piece, (((0,), (0,)), ((), ())), preferred_element_type=jnp.float32
    )


LANES = 128
HALO = 136
PARTS = 2
MESH = pl.DeviceIdType.MESH


def split_np(table):
    high = table.astype(np.float32).astype(jnp.bfloat16)
    low = (table - high.astype(np.float64)).astype(np.float32).astype(jnp.bfloat16)
    return high, low


def spectral_tables(rows):
    span = rows * LANES
    index = np.arange(rows, dtype=np.float64)
    lane = np.arange(LANES, dtype=np.float64)
    first = 2 * np.pi * np.outer(index + 0.25, index) / rows
    twiddle = 2 * np.pi * np.outer(index + 0.25, lane) / span
    second = 2 * np.pi * np.outer(lane, lane) / LANES
    into = np.concatenate([np.cos(first), -np.sin(first)], axis=0)
    high, low = split_np(into)
    into = np.concatenate([high, high, low], axis=1)
    back = np.concatenate([np.cos(first).T, -np.sin(first).T], axis=1) / span
    high, low = split_np(back)
    back = np.concatenate([high, high, low], axis=1)
    cos, sin = np.cos(second), np.sin(second)
    ahead = np.block([[cos, -sin], [sin, cos]])
    ahead = np.stack(split_np(ahead))
    behind = np.block([[cos, sin], [-sin, cos]])
    behind = np.stack(split_np(behind))
    turn = np.stack([np.cos(twiddle), np.sin(twiddle)]).astype(np.float32)
    return into, back, ahead, behind, turn


def split(value):
    high = value.astype(jnp.bfloat16)
    low = (value - high.astype(jnp.float32)).astype(jnp.bfloat16)
    return high, low


def dot(left, right):
    return jnp.dot(left, right, preferred_element_type=jnp.float32)


def dot3(value, table_ref):
    high, low = split(value)
    return dot(high, table_ref[0]) + dot(low, table_ref[0]) + dot(high, table_ref[1])


def to_spectrum(src, spec, each, rows, into_ref, ahead_ref, turn_ref):
    cos, sin = turn_ref[0], turn_ref[1]
    group = 4
    for begin in range(0, each, group):
        lines = [src[pl.ds(begin + i, rows, stride=each), :] for i in range(group)]
        high, low = split(jnp.concatenate(lines, axis=1))
        once = dot(into_ref[...], jnp.concatenate([high, low, high], axis=0))
        turned = []
        for i in range(group):
            real = once[:rows, i * LANES : (i + 1) * LANES]
            imag = once[rows:, i * LANES : (i + 1) * LANES]
            turned.append(
                jnp.concatenate([real * cos + imag * sin, imag * cos - real * sin], axis=1)
            )
        twice = dot3(jnp.concatenate(turned, axis=0), ahead_ref)
        spec[begin * rows : (begin + group) * rows, :] = twice


def from_spectrum(val, filt, dst, each, rows, back_ref, behind_ref, turn_ref):
    cos, sin = turn_ref[0], turn_ref[1]
    group = 4
    for begin in range(0, each, group):
        part = slice(begin * rows, (begin + group) * rows)
        val_real, val_imag = val[part, :LANES], val[part, LANES:]
        filt_real, filt_imag = filt[part, :LANES], filt[part, LANES:]
        product = jnp.concatenate(
            [
                val_real * filt_real - val_imag * filt_imag,
                val_real * filt_imag + val_imag * filt_real,
            ],
            axis=1,
        )
        once = dot3(product, behind_ref)
        turned = []
        for i in range(group):
            real = once[i * rows : (i + 1) * rows, :LANES]
            imag = once[i * rows : (i + 1) * rows, LANES:]
            turned.append(
                jnp.concatenate([real * cos - imag * sin, imag * cos + real * sin], axis=0)
            )
        high, low = split(jnp.concatenate(turned, axis=1))
        lines = dot(back_ref[...], jnp.concatenate([high, low, high], axis=0))
        for i in range(group):
            dst[pl.ds(begin + i, rows, stride=each), :] = lines[:, i * LANES : (i + 1) * LANES]


def kernel(
    seq_size,
    ch_size,
    proj_hbm,
    short_hbm,
    medium_hbm,
    taps_hbm,
    resid_hbm,
    mix_hbm,
    into_hbm,
    back_hbm,
    ahead_hbm,
    behind_hbm,
    turn_hbm,
    out_ref,
    proj_ref,
    short_ref,
    medium_ref,
    taps_ref,
    resid_ref,
    mix_ref,
    into_ref,
    back_ref,
    ahead_ref,
    behind_ref,
    turn_ref,
    stage_sem,
    proj_sem,
    lines_t,
    feat_v,
    taps_out,
    taps_in,
    carrier,
    carrier_in,
    gate,
    answer,
    answer_in,
    spec_filt,
    spec_val,
    gated,
    gathered,
    weights,
    mixed_out,
    mixed_in,
    halo_send,
    halo_recv,
    taps_send,
    taps_recv,
    carrier_send,
    carrier_recv,
    answer_send,
    answer_recv,
    gated_send,
    gated_recv,
    weights_send,
    weights_recv,
    mixed_send,
    mixed_recv,
):
    me = lax.axis_index("seq")
    group = lax.axis_index("ch")
    chan, span = proj_ref.shape[1], proj_ref.shape[2]
    short_span = short_ref.shape[1]
    medium_span = medium_ref.shape[0]
    each = chan // seq_size // PARTS
    blocks = span // LANES
    rows = seq_size * blocks
    slab = blocks * each
    part_chan = chan // PARTS
    share = span // ch_size

    proj_copies = {
        stream: pltpu.make_async_copy(
            proj_hbm.at[stream], proj_ref.at[stream], proj_sem.at[stream]
        )
        for stream in (2, 1, 0)
    }
    staged = {}
    for i, (name, src, dst) in enumerate(
        (
            ("taps", taps_hbm, taps_ref),
            ("short", short_hbm, short_ref),
            ("medium", medium_hbm, medium_ref),
            ("into", into_hbm, into_ref),
            ("turn", turn_hbm, turn_ref),
            ("ahead", ahead_hbm, ahead_ref),
            ("behind", behind_hbm, behind_ref),
            ("back", back_hbm, back_ref),
            ("resid", resid_hbm, resid_ref),
            ("mix", mix_hbm, mix_ref),
        )
    ):
        staged[name] = pltpu.make_async_copy(src, dst, stage_sem.at[i])
    proj_copies[2].start()
    staged["taps"].start()
    proj_copies[1].start()
    proj_copies[0].start()
    for name in staged:
        if name != "taps":
            staged[name].start()

    barrier = pltpu.get_barrier_semaphore()
    for step in range(1, seq_size):
        pl.semaphore_signal(
            barrier, 1, device_id={"seq": lax.rem(me + step, seq_size)}, device_id_type=MESH
        )
    for step in range(1, ch_size):
        pl.semaphore_signal(
            barrier, 1, device_id={"ch": lax.rem(group + step, ch_size)}, device_id_type=MESH
        )

    def transpose_in(stream):
        for k in range(blocks):
            lines_t[stream, HALO + k * LANES : HALO + (k + 1) * LANES, :] = proj_ref[
                stream, :, k * LANES : (k + 1) * LANES
            ].T

    def scatter_rows(dst, k, block):
        for part in range(PARTS):
            for s in range(seq_size):
                begin = s * slab + k * each
                first = part * part_chan + s * each
                dst[part, begin : begin + each, :] = block[first : first + each, :]

    proj_copies[2].wait()
    transpose_in(2)
    staged["taps"].wait()
    for k in range(blocks):
        scatter_rows(taps_out, k, taps_ref[:, k * LANES : (k + 1) * LANES])
    proj_copies[1].wait()
    transpose_in(1)
    proj_copies[0].wait()
    transpose_in(0)
    pl.semaphore_wait(barrier, seq_size - 1 + ch_size - 1)

    def halo_copies():
        after = lax.rem(me + 1, seq_size)
        return [
            pltpu.make_async_remote_copy(
                src_ref=lines_t.at[2, span : span + HALO, :],
                dst_ref=lines_t.at[2, 0:HALO, :],
                send_sem=halo_send.at[0],
                recv_sem=halo_recv.at[0],
                device_id={"seq": after},
                device_id_type=MESH,
            ),
            pltpu.make_async_remote_copy(
                src_ref=lines_t.at[0:2, span + HALO - 8 : span + HALO, :],
                dst_ref=lines_t.at[0:2, HALO - 8 : HALO, :],
                send_sem=halo_send.at[1],
                recv_sem=halo_recv.at[1],
                device_id={"seq": after},
                device_id_type=MESH,
            ),
        ]

    @pl.when(me < seq_size - 1)
    def _():
        for copy in halo_copies():
            copy.start()

    def exchange(src, dst, send, recv, part):
        src, dst, send, recv = src.at[part], dst.at[part], send.at[part], recv.at[part]
        copies = []
        for step in range(1, seq_size):
            peer = lax.rem(me + step, seq_size)
            copies.append(
                pltpu.make_async_remote_copy(
                    src_ref=src.at[pl.ds(pl.multiple_of(peer * slab, 8), slab), :],
                    dst_ref=dst.at[pl.ds(pl.multiple_of(me * slab, 8), slab), :],
                    send_sem=send.at[step],
                    recv_sem=recv.at[step],
                    device_id={"seq": peer},
                    device_id_type=MESH,
                )
            )
        for copy in copies:
            copy.start()
        own = pl.ds(pl.multiple_of(me * slab, 8), slab)
        dst[own, :] = src[own, :]
        return copies

    every = range(PARTS)
    taps_copies = [exchange(taps_out, taps_in, taps_send, taps_recv, part) for part in every]
    staged["short"].wait()
    staged["medium"].wait()
    staged["mix"].wait()
    weight_copies = []
    for step in range(1, ch_size):
        copy = pltpu.make_async_remote_copy(
            src_ref=mix_ref,
            dst_ref=weights.at[group],
            send_sem=weights_send.at[step],
            recv_sem=weights_recv.at[step],
            device_id={"ch": lax.rem(group + step, ch_size)},
            device_id_type=MESH,
        )
        copy.start()
        weight_copies.append(copy)
    weights[group] = mix_ref[...]

    @pl.when(me == 0)
    def _():
        lines_t[2, 0:HALO, :] = jnp.zeros((HALO, chan), jnp.float32)
        lines_t[0:2, HALO - 8 : HALO, :] = jnp.zeros((2, 8, chan), jnp.float32)

    @pl.when(me > 0)
    def _():
        for copy in halo_copies():
            copy.wait_recv()

    def short(stream, begin, count):
        total = None
        for j in range(short_span):
            term = (
                short_ref[stream, j : j + 1, :]
                * lines_t[stream, begin - j : begin - j + count, :]
            )
            total = term if total is None else total + term
        return total

    for begin in range(0, LANES + span, LANES):
        feat_v[begin : begin + LANES, :] = short(2, HALO - LANES + begin, LANES)

    tile = 8

    for k in range(blocks):
        base = (k + 1) * LANES

        def taps_body(m, total):
            for r in range(tile):
                j = m * tile + r
                start = base - r - m * tile
                total = total + medium_ref[pl.ds(j, 1), :] * feat_v[pl.ds(start, LANES), :]
            return total

        smooth = lax.fori_loop(
            0, medium_span // tile, taps_body, jnp.zeros((LANES, chan), jnp.float32)
        )
        block = short(1, HALO + k * LANES, LANES) * smooth
        scatter_rows(carrier, k, block.T)

    carrier_copies = [
        exchange(carrier, carrier_in, carrier_send, carrier_recv, part) for part in every
    ]

    for name in ("into", "turn", "ahead", "behind", "back", "resid"):
        staged[name].wait()
    for part in every:
        for copy in taps_copies[part]:
            copy.wait_recv()
        to_spectrum(
            taps_in.at[part], spec_filt.at[part], each, rows, into_ref, ahead_ref, turn_ref
        )
    for k in range(blocks):
        scatter_rows(gate, k, short(0, HALO + k * LANES, LANES).T)
    resid = jnp.broadcast_to(resid_ref[...], (LANES, chan)).T

    answer_copies = []
    for part in every:
        for copy in carrier_copies[part]:
            copy.wait_recv()
        to_spectrum(carrier_in.at[part], spec_val, each, rows, into_ref, ahead_ref, turn_ref)
        from_spectrum(
            spec_val,
            spec_filt.at[part],
            answer.at[part],
            each,
            rows,
            back_ref,
            behind_ref,
            turn_ref,
        )
        answer_copies.append(exchange(answer, answer_in, answer_send, answer_recv, part))

    gated_copies = []
    for part in every:
        for copy in answer_copies[part]:
            copy.wait_recv()
        for s in range(seq_size):
            first = part * part_chan + s * each
            weight = resid[first : first + each, :]
            for k in range(blocks):
                piece = slice(s * slab + k * each, s * slab + (k + 1) * each)
                value = gate[part, piece, :] * (
                    answer_in[part, piece, :] + weight * carrier[part, piece, :]
                )
                owner, column = divmod(k * LANES, share)
                gated[owner, first : first + each, column : column + LANES] = value.astype(
                    jnp.bfloat16
                )
        lines = slice(part * part_chan, (part + 1) * part_chan)
        for step in range(1, ch_size):
            peer = lax.rem(group + step, ch_size)
            copy = pltpu.make_async_remote_copy(
                src_ref=gated.at[peer, lines, :],
                dst_ref=gathered.at[group, lines, :],
                send_sem=gated_send.at[part, step],
                recv_sem=gated_recv.at[part, step],
                device_id={"ch": peer},
                device_id_type=MESH,
            )
            copy.start()
            gated_copies.append(copy)
        gathered[group, lines, :] = gated[group, lines, :]

    for copy in weight_copies + gated_copies:
        copy.wait_recv()
    signal = gathered[...].reshape(ch_size * chan, share)

    def mixed(owner):
        return lax.dot_general(
            weights[owner], signal, (((0,), (0,)), ((), ())), preferred_element_type=jnp.float32
        )

    mixed_copies = []
    for step in range(1, ch_size):
        peer = lax.rem(group + step, ch_size)
        mixed_out[step] = mixed(peer).astype(jnp.bfloat16)
        copy = pltpu.make_async_remote_copy(
            src_ref=mixed_out.at[step],
            dst_ref=mixed_in.at[group],
            send_sem=mixed_send.at[step],
            recv_sem=mixed_recv.at[step],
            device_id={"ch": peer},
            device_id_type=MESH,
        )
        copy.start()
        mixed_copies.append(copy)
    own = mixed(group)
    for copy in mixed_copies:
        copy.wait_recv()
    for owner in range(ch_size):
        columns = slice(owner * share, (owner + 1) * share)

        @pl.when(group == owner)
        def _():
            out_ref[:, columns] = own

        @pl.when(group != owner)
        def _():
            out_ref[:, columns] = mixed_in[owner].astype(jnp.float32)


    @pl.when(me < seq_size - 1)
    def _():
        for copy in halo_copies():
            copy.wait_send()

    for copies in taps_copies + carrier_copies + answer_copies:
        for copy in copies:
            copy.wait_send()
    for copy in gated_copies + weight_copies + mixed_copies:
        copy.wait_send()


def fused(
    projected, short_taps, medium_taps, global_kernel_taps, residual_coefficient, mixer_weight
):
    seq_size, ch_size = lax.axis_size("seq"), lax.axis_size("ch")
    chan, span = projected.shape[1], projected.shape[2]
    each = chan // seq_size
    rows = seq_size * span // LANES
    tables = [jnp.asarray(table) for table in spectral_tables(rows)]
    vmem = pl.BlockSpec(memory_space=pltpu.VMEM)
    plane = pltpu.VMEM((PARTS, chan * span // LANES // PARTS, LANES), jnp.float32)
    spectrum = (each // PARTS * rows, 2 * LANES)
    dma = pltpu.SemaphoreType.DMA
    operands = (
        projected,
        short_taps.transpose(1, 0, 2),
        medium_taps,
        global_kernel_taps,
        residual_coefficient.reshape(1, chan),
        mixer_weight,
        *tables,
    )
    return pl.pallas_call(
        functools.partial(kernel, seq_size, ch_size),
        out_shape=jax.ShapeDtypeStruct((mixer_weight.shape[1], span), jnp.float32),
        in_specs=[pl.BlockSpec(memory_space=pl.ANY)] * len(operands),
        out_specs=vmem,
        scratch_shapes=[pltpu.VMEM(x.shape, x.dtype) for x in operands]
        + [
            dma((10,)),
            dma((3,)),
            pltpu.VMEM((3, HALO + span, chan), jnp.float32),
            pltpu.VMEM((LANES + span, chan), jnp.float32),
            plane,
            plane,
            plane,
            plane,
            plane,
            plane,
            plane,
            pltpu.VMEM((PARTS, *spectrum), jnp.float32),
            pltpu.VMEM(spectrum, jnp.float32),
            pltpu.VMEM((ch_size, chan, span // ch_size), jnp.bfloat16),
            pltpu.VMEM((ch_size, chan, span // ch_size), jnp.bfloat16),
            pltpu.VMEM((ch_size, *mixer_weight.shape), jnp.bfloat16),
            pltpu.VMEM((ch_size, mixer_weight.shape[1], span // ch_size), jnp.bfloat16),
            pltpu.VMEM((ch_size, mixer_weight.shape[1], span // ch_size), jnp.bfloat16),
            dma((2,)),
            dma((2,)),
            dma((PARTS, seq_size)),
            dma((PARTS, seq_size)),
            dma((PARTS, seq_size)),
            dma((PARTS, seq_size)),
            dma((PARTS, seq_size)),
            dma((PARTS, seq_size)),
            dma((PARTS, ch_size)),
            dma((PARTS, ch_size)),
            dma((ch_size,)),
            dma((ch_size,)),
            dma((ch_size,)),
            dma((ch_size,)),
        ],
        compiler_params=pltpu.CompilerParams(
            collective_id=0, has_side_effects=True, vmem_limit_bytes=60 * 2**20
        ),
        name="hyena",
    )(*operands)


def block(
    projected, short_taps, medium_taps, global_kernel_taps, residual_coefficient, mixer_weight
):
    operands = (
        projected,
        short_taps,
        medium_taps,
        global_kernel_taps,
        residual_coefficient,
        mixer_weight,
    )
    chan, span = projected.shape[1], projected.shape[2]
    each = chan // lax.axis_size("seq")
    fits = (
        chan == LANES
        and span % (LANES * lax.axis_size("ch")) == 0
        and span >= HALO
        and each % 16 == 0
        and medium_taps.shape[0] == LANES
        and short_taps.shape[0] <= 8
        and chan * span * 4 <= 2**20
    )
    return fused(*operands) if fits else shards(*operands)


def solution(mesh):
    return jax.shard_map(
        block,
        mesh=mesh,
        in_specs=(
            P(None, "ch", "seq"),
            P(None, None, "ch"),
            P(None, "ch"),
            P("ch", "seq"),
            P("ch"),
            P(None, "ch"),
        ),
        out_specs=P("ch", "seq"),
        check_vma=False,
    )
```

```python
import functools
import math

import jax
import jax.numpy as jnp
import numpy as np
from jax import lax
from jax.experimental import pallas as pl
from jax.experimental.pallas import tpu as pltpu
from jax.sharding import PartitionSpec as P

HIGHEST = lax.Precision.HIGHEST


def from_behind(shard, axis, by):
    size = lax.axis_size(axis)
    pairs = [(i, i + by) for i in range(size) if 0 <= i + by < size]
    return lax.ppermute(shard, axis, pairs)


def causal_valid(extended, filter_taps, span_out):
    tap_count = filter_taps.shape[0]
    summed = None
    for offset in range(tap_count):
        begin_at = tap_count - 1 - offset
        term = filter_taps[offset][..., None] * extended[..., begin_at : begin_at + span_out]
        summed = term if summed is None else summed + term
    return summed


def square_table(order):
    index = jnp.arange(order, dtype=jnp.int32)
    angle = (index[:, None] * index[None, :] % order).astype(jnp.float32) * (2.0 * math.pi / order)
    return (jnp.cos(angle), jnp.sin(angle))


def make_tables(overall_line_number, adjacent_number):
    first = overall_line_number // 4
    second = 8 * adjacent_number
    padded_len = first * second
    cos_first, sin_first = square_table(first)
    cos_second, sin_second = square_table(second)
    product = (
        jnp.arange(first, dtype=jnp.int32)[:, None] * jnp.arange(second, dtype=jnp.int32)[None, :]
    )
    angle = product.astype(jnp.float32) * (2.0 * math.pi / padded_len)
    return (
        first,
        second,
        padded_len,
        cos_first,
        sin_first,
        cos_second,
        sin_second,
        jnp.cos(angle),
        jnp.sin(angle),
    )


def forward(signal, tables):
    first, second, padded_len, cos_first, sin_first, cos_second, sin_second, twid_cos, twid_sin = (
        tables
    )
    half = first // 2
    blocks = signal.reshape(signal.shape[0], half, second)
    real_one = jnp.einsum("ka,mab->mkb", cos_first[:, :half], blocks, precision=HIGHEST)
    imag_one = -jnp.einsum("ka,mab->mkb", sin_first[:, :half], blocks, precision=HIGHEST)
    real_two = real_one * twid_cos + imag_one * twid_sin
    imag_two = imag_one * twid_cos - real_one * twid_sin
    real_out = jnp.einsum("mkb,bj->mkj", real_two, cos_second, precision=HIGHEST) + jnp.einsum(
        "mkb,bj->mkj", imag_two, sin_second, precision=HIGHEST
    )
    imag_out = jnp.einsum("mkb,bj->mkj", imag_two, cos_second, precision=HIGHEST) - jnp.einsum(
        "mkb,bj->mkj", real_two, sin_second, precision=HIGHEST
    )
    return (real_out, imag_out)


def inverse(spec_real, spec_imag, tables):
    first, second, padded_len, cos_first, sin_first, cos_second, sin_second, twid_cos, twid_sin = (
        tables
    )
    half = first // 2
    real_one = jnp.einsum("mkj,jb->mkb", spec_real, cos_second, precision=HIGHEST) - jnp.einsum(
        "mkj,jb->mkb", spec_imag, sin_second, precision=HIGHEST
    )
    imag_one = jnp.einsum("mkj,jb->mkb", spec_imag, cos_second, precision=HIGHEST) + jnp.einsum(
        "mkj,jb->mkb", spec_real, sin_second, precision=HIGHEST
    )
    real_two = real_one * twid_cos - imag_one * twid_sin
    imag_two = imag_one * twid_cos + real_one * twid_sin
    result = jnp.einsum("ak,mkb->mab", cos_first[:half], real_two, precision=HIGHEST) - jnp.einsum(
        "ak,mkb->mab", sin_first[:half], imag_two, precision=HIGHEST
    )
    return (result / padded_len).reshape(spec_real.shape[0], half * second)


def long_convolve(third_branch_lines, filter_spec, tables):
    val_real, val_imag = forward(third_branch_lines, tables)
    filt_real, filt_imag = filter_spec
    return inverse(
        val_real * filt_real - val_imag * filt_imag,
        val_real * filt_imag + val_imag * filt_real,
        tables,
    )


def shards(
    projected, short_taps, medium_taps, global_kernel_taps, residual_coefficient, mixer_weight
):
    overall_line_number = projected.shape[2]
    chan_local = projected.shape[1]
    adjacent_number = lax.axis_size("seq")
    adjacent_each = chan_local // adjacent_number
    short_span = short_taps.shape[0]
    medium_span = medium_taps.shape[0]
    tables = make_tables(overall_line_number, adjacent_number)
    filter_blocks = global_kernel_taps.reshape(adjacent_number, adjacent_each, overall_line_number)
    short_edge = from_behind(projected[:, :, overall_line_number - (short_span - 1) :], "seq", 1)
    embedded_tokens = causal_valid(
        jnp.concatenate([short_edge, projected], axis=2), short_taps, overall_line_number
    )
    medium_edge = from_behind(
        embedded_tokens[2, :, overall_line_number - (medium_span - 1) :], "seq", 1
    )
    averaged_sequence = causal_valid(
        jnp.concatenate([medium_edge, embedded_tokens[2]], axis=1), medium_taps, overall_line_number
    )
    first_branch_share = embedded_tokens[0]
    second_branch_share = embedded_tokens[1]
    modulating_sequence = second_branch_share * averaged_sequence
    modulating_pieces_array = modulating_sequence.reshape(
        adjacent_number, adjacent_each, overall_line_number
    )
    third_branch_lines = lax.all_to_all(
        modulating_pieces_array, "seq", split_axis=0, concat_axis=2, tiled=True
    )
    filter_piece = lax.all_to_all(filter_blocks, "seq", split_axis=0, concat_axis=2, tiled=True)
    result = long_convolve(third_branch_lines[0], forward(filter_piece[0], tables), tables)
    mixed_response = lax.all_to_all(
        result[None], "seq", split_axis=2, concat_axis=0, tiled=True
    ).reshape(chan_local, overall_line_number)
    multiplied_response = (
        first_branch_share * (mixed_response + residual_coefficient[:, None] * modulating_sequence)
    ).astype(jnp.bfloat16)
    empty = jnp.zeros((mixer_weight.shape[1], overall_line_number), jnp.float32)
    piece = lax.all_gather(multiplied_response, "ch", axis=0, tiled=True)
    weight_rows = lax.slice_in_dim(mixer_weight, 0, piece.shape[0], axis=0)
    return empty + lax.dot_general(
        weight_rows, piece, (((0,), (0,)), ((), ())), preferred_element_type=jnp.float32
    )


LANES = 128
HALO = 136
PARTS = 2
MESH = pl.DeviceIdType.MESH


def split_np(table):
    high = table.astype(np.float32).astype(jnp.bfloat16)
    low = (table - high.astype(np.float64)).astype(np.float32).astype(jnp.bfloat16)
    return high, low


def spectral_tables(rows):
    span = rows * LANES
    index = np.arange(rows, dtype=np.float64)
    lane = np.arange(LANES, dtype=np.float64)
    first = 2 * np.pi * np.outer(index + 0.25, index) / rows
    twiddle = 2 * np.pi * np.outer(index + 0.25, lane) / span
    second = 2 * np.pi * np.outer(lane, lane) / LANES
    into = np.concatenate([np.cos(first), -np.sin(first)], axis=0)
    high, low = split_np(into)
    into = np.concatenate([high, high, low], axis=1)
    back = np.concatenate([np.cos(first).T, -np.sin(first).T], axis=1) / span
    high, low = split_np(back)
    back = np.concatenate([high, high, low], axis=1)
    cos, sin = np.cos(second), np.sin(second)
    ahead = np.block([[cos, -sin], [sin, cos]])
    ahead = np.stack(split_np(ahead))
    behind = np.block([[cos, sin], [-sin, cos]])
    behind = np.stack(split_np(behind))
    turn = np.stack([np.cos(twiddle), np.sin(twiddle)]).astype(np.float32)
    return into, back, ahead, behind, turn


def split(value):
    high = value.astype(jnp.bfloat16)
    low = (value - high.astype(jnp.float32)).astype(jnp.bfloat16)
    return high, low


def dot(left, right):
    return jnp.dot(left, right, preferred_element_type=jnp.float32)


def dot3(value, table_ref):
    high, low = split(value)
    return dot(high, table_ref[0]) + dot(low, table_ref[0]) + dot(high, table_ref[1])


def to_spectrum(src, spec, each, rows, into_ref, ahead_ref, turn_ref):
    cos, sin = turn_ref[0], turn_ref[1]
    group = 4
    for begin in range(0, each, group):
        lines = [src[pl.ds(begin + i, rows, stride=each), :] for i in range(group)]
        high, low = split(jnp.concatenate(lines, axis=1))
        once = dot(into_ref[...], jnp.concatenate([high, low, high], axis=0))
        turned = []
        for i in range(group):
            real = once[:rows, i * LANES : (i + 1) * LANES]
            imag = once[rows:, i * LANES : (i + 1) * LANES]
            turned.append(
                jnp.concatenate([real * cos + imag * sin, imag * cos - real * sin], axis=1)
            )
        twice = dot3(jnp.concatenate(turned, axis=0), ahead_ref)
        spec[begin * rows : (begin + group) * rows, :] = twice


def from_spectrum(val, filt, dst, each, rows, back_ref, behind_ref, turn_ref):
    cos, sin = turn_ref[0], turn_ref[1]
    group = 4
    for begin in range(0, each, group):
        part = slice(begin * rows, (begin + group) * rows)
        val_real, val_imag = val[part, :LANES], val[part, LANES:]
        filt_real, filt_imag = filt[part, :LANES], filt[part, LANES:]
        product = jnp.concatenate(
            [
                val_real * filt_real - val_imag * filt_imag,
                val_real * filt_imag + val_imag * filt_real,
            ],
            axis=1,
        )
        once = dot3(product, behind_ref)
        turned = []
        for i in range(group):
            real = once[i * rows : (i + 1) * rows, :LANES]
            imag = once[i * rows : (i + 1) * rows, LANES:]
            turned.append(
                jnp.concatenate([real * cos - imag * sin, imag * cos + real * sin], axis=0)
            )
        high, low = split(jnp.concatenate(turned, axis=1))
        lines = dot(back_ref[...], jnp.concatenate([high, low, high], axis=0))
        for i in range(group):
            dst[pl.ds(begin + i, rows, stride=each), :] = lines[:, i * LANES : (i + 1) * LANES]


def kernel(
    seq_size,
    ch_size,
    proj_hbm,
    short_hbm,
    medium_hbm,
    taps_hbm,
    resid_hbm,
    mix_hbm,
    into_hbm,
    back_hbm,
    ahead_hbm,
    behind_hbm,
    turn_hbm,
    out_ref,
    proj_ref,
    short_ref,
    medium_ref,
    taps_ref,
    resid_ref,
    mix_ref,
    into_ref,
    back_ref,
    ahead_ref,
    behind_ref,
    turn_ref,
    stage_sem,
    proj_sem,
    lines_t,
    feat_v,
    taps_out,
    taps_in,
    carrier,
    carrier_in,
    gate,
    answer,
    answer_in,
    spec_filt,
    spec_val,
    gated,
    gathered,
    weights,
    mixed_out,
    halo_send,
    halo_recv,
    taps_send,
    taps_recv,
    carrier_send,
    carrier_recv,
    answer_send,
    answer_recv,
    gated_send,
    gated_recv,
    weights_send,
    weights_recv,
    mixed_send,
    mixed_recv,
    own_sem,
):
    me = lax.axis_index("seq")
    group = lax.axis_index("ch")
    chan, span = proj_ref.shape[1], proj_ref.shape[2]
    short_span = short_ref.shape[1]
    medium_span = medium_ref.shape[0]
    each = chan // seq_size // PARTS
    blocks = span // LANES
    rows = seq_size * blocks
    slab = blocks * each
    part_chan = chan // PARTS
    share = span // ch_size

    proj_copies = {
        stream: pltpu.make_async_copy(
            proj_hbm.at[stream], proj_ref.at[stream], proj_sem.at[stream]
        )
        for stream in (2, 1, 0)
    }
    staged = {}
    for i, (name, src, dst) in enumerate(
        (
            ("taps", taps_hbm, taps_ref),
            ("short", short_hbm, short_ref),
            ("medium", medium_hbm, medium_ref),
            ("into", into_hbm, into_ref),
            ("turn", turn_hbm, turn_ref),
            ("ahead", ahead_hbm, ahead_ref),
            ("behind", behind_hbm, behind_ref),
            ("back", back_hbm, back_ref),
            ("resid", resid_hbm, resid_ref),
            ("mix", mix_hbm, mix_ref),
        )
    ):
        staged[name] = pltpu.make_async_copy(src, dst, stage_sem.at[i])
    proj_copies[2].start()
    staged["taps"].start()
    proj_copies[1].start()
    proj_copies[0].start()
    for name in staged:
        if name != "taps":
            staged[name].start()

    barrier = pltpu.get_barrier_semaphore()
    for step in range(1, seq_size):
        pl.semaphore_signal(
            barrier, 1, device_id={"seq": lax.rem(me + step, seq_size)}, device_id_type=MESH
        )
    for step in range(1, ch_size):
        pl.semaphore_signal(
            barrier, 1, device_id={"ch": lax.rem(group + step, ch_size)}, device_id_type=MESH
        )

    def transpose_in(stream):
        for k in range(blocks):
            lines_t[stream, HALO + k * LANES : HALO + (k + 1) * LANES, :] = proj_ref[
                stream, :, k * LANES : (k + 1) * LANES
            ].T

    def scatter_rows(dst, k, block):
        for part in range(PARTS):
            for s in range(seq_size):
                begin = s * slab + k * each
                first = part * part_chan + s * each
                dst[part, begin : begin + each, :] = block[first : first + each, :]

    proj_copies[2].wait()
    transpose_in(2)
    pl.semaphore_wait(barrier, seq_size - 1 + ch_size - 1)

    def halo_copies():
        after = lax.rem(me + 1, seq_size)
        return [
            pltpu.make_async_remote_copy(
                src_ref=lines_t.at[2, span : span + HALO, :],
                dst_ref=lines_t.at[2, 0:HALO, :],
                send_sem=halo_send.at[0],
                recv_sem=halo_recv.at[0],
                device_id={"seq": after},
                device_id_type=MESH,
            ),
            pltpu.make_async_remote_copy(
                src_ref=lines_t.at[0:2, span + HALO - 8 : span + HALO, :],
                dst_ref=lines_t.at[0:2, HALO - 8 : HALO, :],
                send_sem=halo_send.at[1],
                recv_sem=halo_recv.at[1],
                device_id={"seq": after},
                device_id_type=MESH,
            ),
        ]

    @pl.when(me < seq_size - 1)
    def _():
        halo_copies()[0].start()

    def exchange(src, dst, send, recv, part, lane, begin, count):
        src, dst = src.at[part], dst.at[part]
        send, recv = send.at[lane], recv.at[lane]
        copies = []
        for step in range(1, seq_size):
            peer = lax.rem(me + step, seq_size)
            copies.append(
                pltpu.make_async_remote_copy(
                    src_ref=src.at[pl.ds(pl.multiple_of(peer * slab + begin, 8), count), :],
                    dst_ref=dst.at[pl.ds(pl.multiple_of(me * slab + begin, 8), count), :],
                    send_sem=send.at[step],
                    recv_sem=recv.at[step],
                    device_id={"seq": peer},
                    device_id_type=MESH,
                )
            )
        for copy in copies:
            copy.start()
        own = pl.ds(pl.multiple_of(me * slab + begin, 8), count)
        dst[own, :] = src[own, :]
        return copies

    every = range(PARTS)
    proj_copies[1].wait()
    transpose_in(1)
    proj_copies[0].wait()
    transpose_in(0)

    @pl.when(me < seq_size - 1)
    def _():
        halo_copies()[1].start()

    staged["taps"].wait()
    for k in range(blocks):
        scatter_rows(taps_out, k, taps_ref[:, k * LANES : (k + 1) * LANES])
    taps_copies = [
        exchange(taps_out, taps_in, taps_send, taps_recv, part, part, 0, slab) for part in every
    ]
    staged["short"].wait()
    staged["medium"].wait()
    staged["mix"].wait()
    weight_copies = []
    for step in range(1, ch_size):
        copy = pltpu.make_async_remote_copy(
            src_ref=mix_ref,
            dst_ref=weights.at[group],
            send_sem=weights_send.at[step],
            recv_sem=weights_recv.at[step],
            device_id={"ch": lax.rem(group + step, ch_size)},
            device_id_type=MESH,
        )
        copy.start()
        weight_copies.append(copy)
    weights[group] = mix_ref[...]

    def short(stream, begin, count):
        total = None
        for j in range(short_span):
            term = (
                short_ref[stream, j : j + 1, :]
                * lines_t[stream, begin - j : begin - j + count, :]
            )
            total = term if total is None else total + term
        return total

    def featured(begin):
        feat_v[begin : begin + LANES, :] = short(2, HALO - LANES + begin, LANES)

    for begin in range(2 * LANES, LANES + span, LANES):
        featured(begin)

    tile = 8

    def carry(k):
        base = (k + 1) * LANES

        def taps_body(m, total):
            for r in range(tile):
                j = m * tile + r
                start = base - r - m * tile
                total = total + medium_ref[pl.ds(j, 1), :] * feat_v[pl.ds(start, LANES), :]
            return total

        smooth = lax.fori_loop(
            0, medium_span // tile, taps_body, jnp.zeros((LANES, chan), jnp.float32)
        )
        block = short(1, HALO + k * LANES, LANES) * smooth
        scatter_rows(carrier, k, block.T)

    def send_carrier(wave, begin, count):
        return [
            exchange(
                carrier,
                carrier_in,
                carrier_send,
                carrier_recv,
                part,
                part * 2 + wave,
                begin,
                count,
            )
            for part in every
        ]

    for k in range(blocks - 1, 1, -1):
        carry(k)
    early = send_carrier(0, 2 * each, slab - 2 * each)

    @pl.when(me == 0)
    def _():
        lines_t[2, 0:HALO, :] = jnp.zeros((HALO, chan), jnp.float32)
        lines_t[0:2, HALO - 8 : HALO, :] = jnp.zeros((2, 8, chan), jnp.float32)

    @pl.when(me > 0)
    def _():
        for copy in halo_copies():
            copy.wait_recv()

    featured(LANES)
    featured(0)
    carry(1)
    carry(0)
    late = send_carrier(1, 0, 2 * each)
    carrier_copies = [early[part] + late[part] for part in every]

    for name in ("into", "turn", "ahead", "behind", "back", "resid"):
        staged[name].wait()
    for part in every:
        for copy in taps_copies[part]:
            copy.wait_recv()
        to_spectrum(
            taps_in.at[part], spec_filt.at[part], each, rows, into_ref, ahead_ref, turn_ref
        )
    for k in range(blocks):
        scatter_rows(gate, k, short(0, HALO + k * LANES, LANES).T)
    resid = jnp.broadcast_to(resid_ref[...], (LANES, chan)).T

    answer_copies = []
    for part in every:
        for copy in carrier_copies[part]:
            copy.wait_recv()
        to_spectrum(carrier_in.at[part], spec_val, each, rows, into_ref, ahead_ref, turn_ref)
        from_spectrum(
            spec_val,
            spec_filt.at[part],
            answer.at[part],
            each,
            rows,
            back_ref,
            behind_ref,
            turn_ref,
        )
        answer_copies.append(exchange(answer, answer_in, answer_send, answer_recv, part, part, 0, slab))

    gated_copies = []
    for part in every:
        for copy in answer_copies[part]:
            copy.wait_recv()
        for s in range(seq_size):
            first = part * part_chan + s * each
            weight = resid[first : first + each, :]
            for k in range(blocks):
                piece = slice(s * slab + k * each, s * slab + (k + 1) * each)
                value = gate[part, piece, :] * (
                    answer_in[part, piece, :] + weight * carrier[part, piece, :]
                )
                owner, column = divmod(k * LANES, share)
                gated[owner, first : first + each, column : column + LANES] = value.astype(
                    jnp.bfloat16
                )
        lines = slice(part * part_chan, (part + 1) * part_chan)
        for step in range(1, ch_size):
            peer = lax.rem(group + step, ch_size)
            copy = pltpu.make_async_remote_copy(
                src_ref=gated.at[peer, lines, :],
                dst_ref=gathered.at[group, lines, :],
                send_sem=gated_send.at[part, step],
                recv_sem=gated_recv.at[part, step],
                device_id={"ch": peer},
                device_id_type=MESH,
            )
            copy.start()
            gated_copies.append(copy)
        gathered[group, lines, :] = gated[group, lines, :]

    for copy in weight_copies + gated_copies:
        copy.wait_recv()
    signal = gathered[...].reshape(ch_size * chan, share)

    def mixed(owner):
        return lax.dot_general(
            weights[owner], signal, (((0,), (0,)), ((), ())), preferred_element_type=jnp.float32
        )

    mine = pl.ds(pl.multiple_of(group * share, LANES), share)
    mixed_copies = []
    for step in range(1, ch_size):
        peer = lax.rem(group + step, ch_size)
        mixed_out[step] = mixed(peer).astype(jnp.bfloat16)
        copy = pltpu.make_async_remote_copy(
            src_ref=mixed_out.at[step],
            dst_ref=out_ref.at[:, mine],
            send_sem=mixed_send.at[step],
            recv_sem=mixed_recv.at[step],
            device_id={"ch": peer},
            device_id_type=MESH,
        )
        copy.start()
        mixed_copies.append(copy)
    mixed_out[0] = mixed(group).astype(jnp.bfloat16)
    own = pltpu.make_async_copy(mixed_out.at[0], out_ref.at[:, mine], own_sem)
    own.start()
    for copy in mixed_copies:
        copy.wait_recv()
    own.wait()

    @pl.when(me < seq_size - 1)
    def _():
        for copy in halo_copies():
            copy.wait_send()

    for copies in taps_copies + carrier_copies + answer_copies:
        for copy in copies:
            copy.wait_send()
    for copy in gated_copies + weight_copies + mixed_copies:
        copy.wait_send()


def fused(
    projected, short_taps, medium_taps, global_kernel_taps, residual_coefficient, mixer_weight
):
    seq_size, ch_size = lax.axis_size("seq"), lax.axis_size("ch")
    chan, span = projected.shape[1], projected.shape[2]
    each = chan // seq_size
    rows = seq_size * span // LANES
    tables = [jnp.asarray(table) for table in spectral_tables(rows)]
    plane = pltpu.VMEM((PARTS, chan * span // LANES // PARTS, LANES), jnp.float32)
    spectrum = (each // PARTS * rows, 2 * LANES)
    dma = pltpu.SemaphoreType.DMA
    operands = (
        projected,
        short_taps.transpose(1, 0, 2),
        medium_taps,
        global_kernel_taps,
        residual_coefficient.reshape(1, chan),
        mixer_weight,
        *tables,
    )
    mixed = pl.pallas_call(
        functools.partial(kernel, seq_size, ch_size),
        out_shape=jax.ShapeDtypeStruct((mixer_weight.shape[1], span), jnp.bfloat16),
        in_specs=[pl.BlockSpec(memory_space=pl.ANY)] * len(operands),
        out_specs=pl.BlockSpec(memory_space=pl.ANY),
        scratch_shapes=[pltpu.VMEM(x.shape, x.dtype) for x in operands]
        + [
            dma((10,)),
            dma((3,)),
            pltpu.VMEM((3, HALO + span, chan), jnp.float32),
            pltpu.VMEM((LANES + span, chan), jnp.float32),
            plane,
            plane,
            plane,
            plane,
            plane,
            plane,
            plane,
            pltpu.VMEM((PARTS, *spectrum), jnp.float32),
            pltpu.VMEM(spectrum, jnp.float32),
            pltpu.VMEM((ch_size, chan, span // ch_size), jnp.bfloat16),
            pltpu.VMEM((ch_size, chan, span // ch_size), jnp.bfloat16),
            pltpu.VMEM((ch_size, *mixer_weight.shape), jnp.bfloat16),
            pltpu.VMEM((ch_size, mixer_weight.shape[1], span // ch_size), jnp.bfloat16),
            dma((2,)),
            dma((2,)),
            dma((PARTS, seq_size)),
            dma((PARTS, seq_size)),
            dma((PARTS * 2, seq_size)),
            dma((PARTS * 2, seq_size)),
            dma((PARTS, seq_size)),
            dma((PARTS, seq_size)),
            dma((PARTS, ch_size)),
            dma((PARTS, ch_size)),
            dma((ch_size,)),
            dma((ch_size,)),
            dma((ch_size,)),
            dma((ch_size,)),
            dma(()),
        ],
        compiler_params=pltpu.CompilerParams(
            collective_id=0, has_side_effects=True, vmem_limit_bytes=60 * 2**20
        ),
        name="hyena",
    )(*operands)
    return mixed.astype(jnp.float32)


def block(
    projected, short_taps, medium_taps, global_kernel_taps, residual_coefficient, mixer_weight
):
    operands = (
        projected,
        short_taps,
        medium_taps,
        global_kernel_taps,
        residual_coefficient,
        mixer_weight,
    )
    chan, span = projected.shape[1], projected.shape[2]
    each = chan // lax.axis_size("seq")
    fits = (
        chan == LANES
        and span % (LANES * lax.axis_size("ch")) == 0
        and span >= HALO
        and each % 16 == 0
        and medium_taps.shape[0] == LANES
        and short_taps.shape[0] <= 8
        and chan * span * 4 <= 2**20
    )
    return fused(*operands) if fits else shards(*operands)


def solution(mesh):
    return jax.shard_map(
        block,
        mesh=mesh,
        in_specs=(
            P(None, "ch", "seq"),
            P(None, None, "ch"),
            P(None, "ch"),
            P("ch", "seq"),
            P("ch"),
            P(None, "ch"),
        ),
        out_specs=P("ch", "seq"),
        check_vma=False,
    )
```

```python
import functools
import math

import jax
import jax.numpy as jnp
import numpy as np
from jax import lax
from jax.experimental import pallas as pl
from jax.experimental.pallas import tpu as pltpu
from jax.sharding import PartitionSpec as P

HIGHEST = lax.Precision.HIGHEST


def from_behind(shard, axis, by):
    size = lax.axis_size(axis)
    pairs = [(i, i + by) for i in range(size) if 0 <= i + by < size]
    return lax.ppermute(shard, axis, pairs)


def causal_valid(extended, filter_taps, span_out):
    tap_count = filter_taps.shape[0]
    summed = None
    for offset in range(tap_count):
        begin_at = tap_count - 1 - offset
        term = filter_taps[offset][..., None] * extended[..., begin_at : begin_at + span_out]
        summed = term if summed is None else summed + term
    return summed


def square_table(order):
    index = jnp.arange(order, dtype=jnp.int32)
    angle = (index[:, None] * index[None, :] % order).astype(jnp.float32) * (2.0 * math.pi / order)
    return (jnp.cos(angle), jnp.sin(angle))


def make_tables(overall_line_number, adjacent_number):
    first = overall_line_number // 4
    second = 8 * adjacent_number
    padded_len = first * second
    cos_first, sin_first = square_table(first)
    cos_second, sin_second = square_table(second)
    product = (
        jnp.arange(first, dtype=jnp.int32)[:, None] * jnp.arange(second, dtype=jnp.int32)[None, :]
    )
    angle = product.astype(jnp.float32) * (2.0 * math.pi / padded_len)
    return (
        first,
        second,
        padded_len,
        cos_first,
        sin_first,
        cos_second,
        sin_second,
        jnp.cos(angle),
        jnp.sin(angle),
    )


def forward(signal, tables):
    first, second, padded_len, cos_first, sin_first, cos_second, sin_second, twid_cos, twid_sin = (
        tables
    )
    half = first // 2
    blocks = signal.reshape(signal.shape[0], half, second)
    real_one = jnp.einsum("ka,mab->mkb", cos_first[:, :half], blocks, precision=HIGHEST)
    imag_one = -jnp.einsum("ka,mab->mkb", sin_first[:, :half], blocks, precision=HIGHEST)
    real_two = real_one * twid_cos + imag_one * twid_sin
    imag_two = imag_one * twid_cos - real_one * twid_sin
    real_out = jnp.einsum("mkb,bj->mkj", real_two, cos_second, precision=HIGHEST) + jnp.einsum(
        "mkb,bj->mkj", imag_two, sin_second, precision=HIGHEST
    )
    imag_out = jnp.einsum("mkb,bj->mkj", imag_two, cos_second, precision=HIGHEST) - jnp.einsum(
        "mkb,bj->mkj", real_two, sin_second, precision=HIGHEST
    )
    return (real_out, imag_out)


def inverse(spec_real, spec_imag, tables):
    first, second, padded_len, cos_first, sin_first, cos_second, sin_second, twid_cos, twid_sin = (
        tables
    )
    half = first // 2
    real_one = jnp.einsum("mkj,jb->mkb", spec_real, cos_second, precision=HIGHEST) - jnp.einsum(
        "mkj,jb->mkb", spec_imag, sin_second, precision=HIGHEST
    )
    imag_one = jnp.einsum("mkj,jb->mkb", spec_imag, cos_second, precision=HIGHEST) + jnp.einsum(
        "mkj,jb->mkb", spec_real, sin_second, precision=HIGHEST
    )
    real_two = real_one * twid_cos - imag_one * twid_sin
    imag_two = imag_one * twid_cos + real_one * twid_sin
    result = jnp.einsum("ak,mkb->mab", cos_first[:half], real_two, precision=HIGHEST) - jnp.einsum(
        "ak,mkb->mab", sin_first[:half], imag_two, precision=HIGHEST
    )
    return (result / padded_len).reshape(spec_real.shape[0], half * second)


def long_convolve(third_branch_lines, filter_spec, tables):
    val_real, val_imag = forward(third_branch_lines, tables)
    filt_real, filt_imag = filter_spec
    return inverse(
        val_real * filt_real - val_imag * filt_imag,
        val_real * filt_imag + val_imag * filt_real,
        tables,
    )


def shards(
    projected, short_taps, medium_taps, global_kernel_taps, residual_coefficient, mixer_weight
):
    overall_line_number = projected.shape[2]
    chan_local = projected.shape[1]
    adjacent_number = lax.axis_size("seq")
    adjacent_each = chan_local // adjacent_number
    short_span = short_taps.shape[0]
    medium_span = medium_taps.shape[0]
    tables = make_tables(overall_line_number, adjacent_number)
    filter_blocks = global_kernel_taps.reshape(adjacent_number, adjacent_each, overall_line_number)
    short_edge = from_behind(projected[:, :, overall_line_number - (short_span - 1) :], "seq", 1)
    embedded_tokens = causal_valid(
        jnp.concatenate([short_edge, projected], axis=2), short_taps, overall_line_number
    )
    medium_edge = from_behind(
        embedded_tokens[2, :, overall_line_number - (medium_span - 1) :], "seq", 1
    )
    averaged_sequence = causal_valid(
        jnp.concatenate([medium_edge, embedded_tokens[2]], axis=1), medium_taps, overall_line_number
    )
    first_branch_share = embedded_tokens[0]
    second_branch_share = embedded_tokens[1]
    modulating_sequence = second_branch_share * averaged_sequence
    modulating_pieces_array = modulating_sequence.reshape(
        adjacent_number, adjacent_each, overall_line_number
    )
    third_branch_lines = lax.all_to_all(
        modulating_pieces_array, "seq", split_axis=0, concat_axis=2, tiled=True
    )
    filter_piece = lax.all_to_all(filter_blocks, "seq", split_axis=0, concat_axis=2, tiled=True)
    result = long_convolve(third_branch_lines[0], forward(filter_piece[0], tables), tables)
    mixed_response = lax.all_to_all(
        result[None], "seq", split_axis=2, concat_axis=0, tiled=True
    ).reshape(chan_local, overall_line_number)
    multiplied_response = (
        first_branch_share * (mixed_response + residual_coefficient[:, None] * modulating_sequence)
    ).astype(jnp.bfloat16)
    empty = jnp.zeros((mixer_weight.shape[1], overall_line_number), jnp.float32)
    piece = lax.all_gather(multiplied_response, "ch", axis=0, tiled=True)
    weight_rows = lax.slice_in_dim(mixer_weight, 0, piece.shape[0], axis=0)
    return empty + lax.dot_general(
        weight_rows, piece, (((0,), (0,)), ((), ())), preferred_element_type=jnp.float32
    )


LANES = 128
HALO = 136
PARTS = 2
MESH = pl.DeviceIdType.MESH


def split_np(table):
    high = table.astype(np.float32).astype(jnp.bfloat16)
    low = (table - high.astype(np.float64)).astype(np.float32).astype(jnp.bfloat16)
    return high, low


def spectral_tables(rows):
    span = rows * LANES
    index = np.arange(rows, dtype=np.float64)
    lane = np.arange(LANES, dtype=np.float64)
    first = 2 * np.pi * np.outer(index + 0.25, index) / rows
    twiddle = 2 * np.pi * np.outer(index + 0.25, lane) / span
    second = 2 * np.pi * np.outer(lane, lane) / LANES
    into = np.concatenate([np.cos(first), -np.sin(first)], axis=0)
    high, low = split_np(into)
    into = np.concatenate([high, high, low], axis=1)
    back = np.concatenate([np.cos(first).T, -np.sin(first).T], axis=1) / span
    high, low = split_np(back)
    back = np.concatenate([high, high, low], axis=1)
    cos, sin = np.cos(second), np.sin(second)
    ahead = np.block([[cos, -sin], [sin, cos]])
    ahead = np.stack(split_np(ahead))
    behind = np.block([[cos, sin], [-sin, cos]])
    behind = np.stack(split_np(behind))
    turn = np.stack([np.cos(twiddle), np.sin(twiddle)]).astype(np.float32)
    return into, back, ahead, behind, turn


def split(value):
    high = value.astype(jnp.bfloat16)
    low = (value - high.astype(jnp.float32)).astype(jnp.bfloat16)
    return high, low


def dot(left, right):
    return jnp.dot(left, right, preferred_element_type=jnp.float32)


def dot3(value, table_ref):
    high, low = split(value)
    return dot(high, table_ref[0]) + dot(low, table_ref[0]) + dot(high, table_ref[1])


def to_spectrum(src, spec, each, rows, into_ref, ahead_ref, turn_ref):
    cos, sin = turn_ref[0], turn_ref[1]
    group = 4
    for begin in range(0, each, group):
        lines = [src[pl.ds(begin + i, rows, stride=each), :] for i in range(group)]
        high, low = split(jnp.concatenate(lines, axis=1))
        once = dot(into_ref[...], jnp.concatenate([high, low, high], axis=0))
        turned = []
        for i in range(group):
            real = once[:rows, i * LANES : (i + 1) * LANES]
            imag = once[rows:, i * LANES : (i + 1) * LANES]
            turned.append(
                jnp.concatenate([real * cos + imag * sin, imag * cos - real * sin], axis=1)
            )
        twice = dot3(jnp.concatenate(turned, axis=0), ahead_ref)
        spec[begin * rows : (begin + group) * rows, :] = twice


def from_spectrum(val, filt, dst, each, rows, back_ref, behind_ref, turn_ref):
    cos, sin = turn_ref[0], turn_ref[1]
    group = 4
    for begin in range(0, each, group):
        part = slice(begin * rows, (begin + group) * rows)
        val_real, val_imag = val[part, :LANES], val[part, LANES:]
        filt_real, filt_imag = filt[part, :LANES], filt[part, LANES:]
        product = jnp.concatenate(
            [
                val_real * filt_real - val_imag * filt_imag,
                val_real * filt_imag + val_imag * filt_real,
            ],
            axis=1,
        )
        once = dot3(product, behind_ref)
        turned = []
        for i in range(group):
            real = once[i * rows : (i + 1) * rows, :LANES]
            imag = once[i * rows : (i + 1) * rows, LANES:]
            turned.append(
                jnp.concatenate([real * cos - imag * sin, imag * cos + real * sin], axis=0)
            )
        high, low = split(jnp.concatenate(turned, axis=1))
        lines = dot(back_ref[...], jnp.concatenate([high, low, high], axis=0))
        for i in range(group):
            dst[pl.ds(begin + i, rows, stride=each), :] = lines[:, i * LANES : (i + 1) * LANES]


def kernel(
    seq_size,
    ch_size,
    proj_hbm,
    short_hbm,
    medium_hbm,
    taps_hbm,
    resid_hbm,
    mix_hbm,
    into_hbm,
    back_hbm,
    ahead_hbm,
    behind_hbm,
    turn_hbm,
    out_ref,
    proj_ref,
    short_ref,
    medium_ref,
    taps_ref,
    resid_ref,
    mix_ref,
    into_ref,
    back_ref,
    ahead_ref,
    behind_ref,
    turn_ref,
    stage_sem,
    proj_sem,
    lines_t,
    feat_v,
    taps_out,
    taps_in,
    carrier,
    carrier_in,
    gate,
    answer,
    answer_in,
    spec_filt,
    spec_val,
    gated,
    gathered,
    weights,
    turned_weights,
    mixed_out,
    halo_send,
    halo_recv,
    taps_send,
    taps_recv,
    carrier_send,
    carrier_recv,
    answer_send,
    answer_recv,
    gated_send,
    gated_recv,
    weights_send,
    weights_recv,
    mixed_send,
    mixed_recv,
    own_sem,
):
    me = lax.axis_index("seq")
    group = lax.axis_index("ch")
    chan, span = proj_ref.shape[1], proj_ref.shape[2]
    short_span = short_ref.shape[1]
    medium_span = medium_ref.shape[0]
    each = chan // seq_size // PARTS
    blocks = span // LANES
    rows = seq_size * blocks
    slab = blocks * each
    part_chan = chan // PARTS
    share = span // ch_size

    proj_copies = {
        stream: pltpu.make_async_copy(
            proj_hbm.at[stream], proj_ref.at[stream], proj_sem.at[stream]
        )
        for stream in (2, 1, 0)
    }
    staged = {}
    for i, (name, src, dst) in enumerate(
        (
            ("taps", taps_hbm, taps_ref),
            ("short", short_hbm, short_ref),
            ("medium", medium_hbm, medium_ref),
            ("into", into_hbm, into_ref),
            ("turn", turn_hbm, turn_ref),
            ("ahead", ahead_hbm, ahead_ref),
            ("behind", behind_hbm, behind_ref),
            ("back", back_hbm, back_ref),
            ("resid", resid_hbm, resid_ref),
            ("mix", mix_hbm, mix_ref),
        )
    ):
        staged[name] = pltpu.make_async_copy(src, dst, stage_sem.at[i])
    proj_copies[2].start()
    staged["taps"].start()
    proj_copies[1].start()
    proj_copies[0].start()
    for name in staged:
        if name != "taps":
            staged[name].start()

    barrier = pltpu.get_barrier_semaphore()
    for step in range(1, seq_size):
        pl.semaphore_signal(
            barrier, 1, device_id={"seq": lax.rem(me + step, seq_size)}, device_id_type=MESH
        )
    for step in range(1, ch_size):
        pl.semaphore_signal(
            barrier, 1, device_id={"ch": lax.rem(group + step, ch_size)}, device_id_type=MESH
        )

    def transpose_in(stream):
        for k in range(blocks):
            lines_t[stream, HALO + k * LANES : HALO + (k + 1) * LANES, :] = proj_ref[
                stream, :, k * LANES : (k + 1) * LANES
            ].T

    def scatter_rows(dst, k, block):
        for part in range(PARTS):
            for s in range(seq_size):
                begin = s * slab + k * each
                first = part * part_chan + s * each
                dst[part, begin : begin + each, :] = block[first : first + each, :]

    proj_copies[2].wait()
    transpose_in(2)
    pl.semaphore_wait(barrier, seq_size - 1 + ch_size - 1)

    def halo_copies():
        after = lax.rem(me + 1, seq_size)
        return [
            pltpu.make_async_remote_copy(
                src_ref=lines_t.at[2, span : span + HALO, :],
                dst_ref=lines_t.at[2, 0:HALO, :],
                send_sem=halo_send.at[0],
                recv_sem=halo_recv.at[0],
                device_id={"seq": after},
                device_id_type=MESH,
            ),
            pltpu.make_async_remote_copy(
                src_ref=lines_t.at[0:2, span + HALO - 8 : span + HALO, :],
                dst_ref=lines_t.at[0:2, HALO - 8 : HALO, :],
                send_sem=halo_send.at[1],
                recv_sem=halo_recv.at[1],
                device_id={"seq": after},
                device_id_type=MESH,
            ),
        ]

    @pl.when(me < seq_size - 1)
    def _():
        halo_copies()[0].start()

    def exchange(src, dst, send, recv, part, lane, begin, count):
        src, dst = src.at[part], dst.at[part]
        send, recv = send.at[lane], recv.at[lane]
        copies = []
        for step in range(1, seq_size):
            peer = lax.rem(me + step, seq_size)
            copies.append(
                pltpu.make_async_remote_copy(
                    src_ref=src.at[pl.ds(pl.multiple_of(peer * slab + begin, 8), count), :],
                    dst_ref=dst.at[pl.ds(pl.multiple_of(me * slab + begin, 8), count), :],
                    send_sem=send.at[step],
                    recv_sem=recv.at[step],
                    device_id={"seq": peer},
                    device_id_type=MESH,
                )
            )
        for copy in copies:
            copy.start()
        own = pl.ds(pl.multiple_of(me * slab + begin, 8), count)
        dst[own, :] = src[own, :]
        return copies

    every = range(PARTS)
    proj_copies[1].wait()
    transpose_in(1)
    proj_copies[0].wait()
    transpose_in(0)

    @pl.when(me < seq_size - 1)
    def _():
        halo_copies()[1].start()

    staged["taps"].wait()
    for k in range(blocks):
        scatter_rows(taps_out, k, taps_ref[:, k * LANES : (k + 1) * LANES])
    taps_copies = [
        exchange(taps_out, taps_in, taps_send, taps_recv, part, part, 0, slab) for part in every
    ]
    staged["short"].wait()
    staged["medium"].wait()
    staged["mix"].wait()
    weight_copies = []
    for step in range(1, ch_size):
        copy = pltpu.make_async_remote_copy(
            src_ref=mix_ref,
            dst_ref=weights.at[group],
            send_sem=weights_send.at[step],
            recv_sem=weights_recv.at[step],
            device_id={"ch": lax.rem(group + step, ch_size)},
            device_id_type=MESH,
        )
        copy.start()
        weight_copies.append(copy)
    weights[group] = mix_ref[...]

    def short(stream, begin, count):
        total = None
        for j in range(short_span):
            term = (
                short_ref[stream, j : j + 1, :]
                * lines_t[stream, begin - j : begin - j + count, :]
            )
            total = term if total is None else total + term
        return total

    def featured(begin):
        feat_v[begin : begin + LANES, :] = short(2, HALO - LANES + begin, LANES)

    for begin in range(2 * LANES, LANES + span, LANES):
        featured(begin)

    tile = 8

    def carry(k):
        base = (k + 1) * LANES

        def taps_body(m, total):
            for r in range(tile):
                j = m * tile + r
                start = base - r - m * tile
                total = total + medium_ref[pl.ds(j, 1), :] * feat_v[pl.ds(start, LANES), :]
            return total

        smooth = lax.fori_loop(
            0, medium_span // tile, taps_body, jnp.zeros((LANES, chan), jnp.float32)
        )
        block = short(1, HALO + k * LANES, LANES) * smooth
        scatter_rows(carrier, k, block.T)

    def send_carrier(wave, begin, count):
        return [
            exchange(
                carrier,
                carrier_in,
                carrier_send,
                carrier_recv,
                part,
                part * 2 + wave,
                begin,
                count,
            )
            for part in every
        ]

    for k in range(blocks - 1, 1, -1):
        carry(k)
    early = send_carrier(0, 2 * each, slab - 2 * each)

    @pl.when(me == 0)
    def _():
        lines_t[2, 0:HALO, :] = jnp.zeros((HALO, chan), jnp.float32)
        lines_t[0:2, HALO - 8 : HALO, :] = jnp.zeros((2, 8, chan), jnp.float32)

    @pl.when(me > 0)
    def _():
        for copy in halo_copies():
            copy.wait_recv()

    featured(LANES)
    featured(0)
    carry(1)
    carry(0)
    late = send_carrier(1, 0, 2 * each)
    carrier_copies = [early[part] + late[part] for part in every]

    for name in ("into", "turn", "ahead", "behind", "back", "resid"):
        staged[name].wait()
    for part in every:
        for copy in taps_copies[part]:
            copy.wait_recv()
        to_spectrum(
            taps_in.at[part], spec_filt.at[part], each, rows, into_ref, ahead_ref, turn_ref
        )
    for k in range(blocks):
        scatter_rows(gate, k, short(0, HALO + k * LANES, LANES).T)
    resid = jnp.broadcast_to(resid_ref[...], (LANES, chan)).T

    answer_copies = []
    for part in every:
        for copy in carrier_copies[part]:
            copy.wait_recv()
        to_spectrum(carrier_in.at[part], spec_val, each, rows, into_ref, ahead_ref, turn_ref)
        from_spectrum(
            spec_val,
            spec_filt.at[part],
            answer.at[part],
            each,
            rows,
            back_ref,
            behind_ref,
            turn_ref,
        )
        answer_copies.append(exchange(answer, answer_in, answer_send, answer_recv, part, part, 0, slab))

    for copy in weight_copies:
        copy.wait_recv()
    for owner in range(ch_size):
        turned_weights[owner] = weights[owner].astype(jnp.float32).T.astype(jnp.bfloat16)

    gated_copies = []
    for part in every:
        for copy in answer_copies[part]:
            copy.wait_recv()
        for s in range(seq_size):
            first = part * part_chan + s * each
            weight = resid[first : first + each, :]
            for k in range(blocks):
                piece = slice(s * slab + k * each, s * slab + (k + 1) * each)
                value = gate[part, piece, :] * (
                    answer_in[part, piece, :] + weight * carrier[part, piece, :]
                )
                owner, column = divmod(k * LANES, share)
                gated[owner, first : first + each, column : column + LANES] = value.astype(
                    jnp.bfloat16
                )
        lines = slice(part * part_chan, (part + 1) * part_chan)
        for step in range(1, ch_size):
            peer = lax.rem(group + step, ch_size)
            copy = pltpu.make_async_remote_copy(
                src_ref=gated.at[peer, lines, :],
                dst_ref=gathered.at[group, lines, :],
                send_sem=gated_send.at[part, step],
                recv_sem=gated_recv.at[part, step],
                device_id={"ch": peer},
                device_id_type=MESH,
            )
            copy.start()
            gated_copies.append(copy)
        gathered[group, lines, :] = gated[group, lines, :]

    for copy in gated_copies:
        copy.wait_recv()
    signal = gathered[...].reshape(ch_size * chan, share)

    def mixed(owner):
        return dot(turned_weights[owner], signal)

    mine = pl.ds(pl.multiple_of(group * share, LANES), share)
    mixed_copies = []
    for step in range(1, ch_size):
        peer = lax.rem(group + step, ch_size)
        mixed_out[step] = mixed(peer).astype(jnp.bfloat16)
        copy = pltpu.make_async_remote_copy(
            src_ref=mixed_out.at[step],
            dst_ref=out_ref.at[:, mine],
            send_sem=mixed_send.at[step],
            recv_sem=mixed_recv.at[step],
            device_id={"ch": peer},
            device_id_type=MESH,
        )
        copy.start()
        mixed_copies.append(copy)
    mixed_out[0] = mixed(group).astype(jnp.bfloat16)
    own = pltpu.make_async_copy(mixed_out.at[0], out_ref.at[:, mine], own_sem)
    own.start()
    for copy in mixed_copies:
        copy.wait_recv()
    own.wait()

    @pl.when(me < seq_size - 1)
    def _():
        for copy in halo_copies():
            copy.wait_send()

    for copies in taps_copies + carrier_copies + answer_copies:
        for copy in copies:
            copy.wait_send()
    for copy in gated_copies + weight_copies + mixed_copies:
        copy.wait_send()


def fused(
    projected, short_taps, medium_taps, global_kernel_taps, residual_coefficient, mixer_weight
):
    seq_size, ch_size = lax.axis_size("seq"), lax.axis_size("ch")
    chan, span = projected.shape[1], projected.shape[2]
    each = chan // seq_size
    rows = seq_size * span // LANES
    tables = [jnp.asarray(table) for table in spectral_tables(rows)]
    plane = pltpu.VMEM((PARTS, chan * span // LANES // PARTS, LANES), jnp.float32)
    spectrum = (each // PARTS * rows, 2 * LANES)
    dma = pltpu.SemaphoreType.DMA
    operands = (
        projected,
        short_taps.transpose(1, 0, 2),
        medium_taps,
        global_kernel_taps,
        residual_coefficient.reshape(1, chan),
        mixer_weight,
        *tables,
    )
    mixed = pl.pallas_call(
        functools.partial(kernel, seq_size, ch_size),
        out_shape=jax.ShapeDtypeStruct((mixer_weight.shape[1], span), jnp.bfloat16),
        in_specs=[pl.BlockSpec(memory_space=pl.ANY)] * len(operands),
        out_specs=pl.BlockSpec(memory_space=pl.ANY),
        scratch_shapes=[pltpu.VMEM(x.shape, x.dtype) for x in operands]
        + [
            dma((10,)),
            dma((3,)),
            pltpu.VMEM((3, HALO + span, chan), jnp.float32),
            pltpu.VMEM((LANES + span, chan), jnp.float32),
            plane,
            plane,
            plane,
            plane,
            plane,
            plane,
            plane,
            pltpu.VMEM((PARTS, *spectrum), jnp.float32),
            pltpu.VMEM(spectrum, jnp.float32),
            pltpu.VMEM((ch_size, chan, span // ch_size), jnp.bfloat16),
            pltpu.VMEM((ch_size, chan, span // ch_size), jnp.bfloat16),
            pltpu.VMEM((ch_size, *mixer_weight.shape), jnp.bfloat16),
            pltpu.VMEM((ch_size, *mixer_weight.shape[::-1]), jnp.bfloat16),
            pltpu.VMEM((ch_size, mixer_weight.shape[1], span // ch_size), jnp.bfloat16),
            dma((2,)),
            dma((2,)),
            dma((PARTS, seq_size)),
            dma((PARTS, seq_size)),
            dma((PARTS * 2, seq_size)),
            dma((PARTS * 2, seq_size)),
            dma((PARTS, seq_size)),
            dma((PARTS, seq_size)),
            dma((PARTS, ch_size)),
            dma((PARTS, ch_size)),
            dma((ch_size,)),
            dma((ch_size,)),
            dma((ch_size,)),
            dma((ch_size,)),
            dma(()),
        ],
        compiler_params=pltpu.CompilerParams(
            collective_id=0, has_side_effects=True, vmem_limit_bytes=60 * 2**20
        ),
        name="hyena",
    )(*operands)
    return mixed.astype(jnp.float32)


def block(
    projected, short_taps, medium_taps, global_kernel_taps, residual_coefficient, mixer_weight
):
    operands = (
        projected,
        short_taps,
        medium_taps,
        global_kernel_taps,
        residual_coefficient,
        mixer_weight,
    )
    chan, span = projected.shape[1], projected.shape[2]
    each = chan // lax.axis_size("seq")
    fits = (
        chan == LANES
        and span % (LANES * lax.axis_size("ch")) == 0
        and span >= HALO
        and each % 16 == 0
        and medium_taps.shape[0] == LANES
        and short_taps.shape[0] <= 8
        and chan * span * 4 <= 2**20
    )
    return fused(*operands) if fits else shards(*operands)


def solution(mesh):
    return jax.shard_map(
        block,
        mesh=mesh,
        in_specs=(
            P(None, "ch", "seq"),
            P(None, None, "ch"),
            P(None, "ch"),
            P("ch", "seq"),
            P("ch"),
            P(None, "ch"),
        ),
        out_specs=P("ch", "seq"),
        check_vma=False,
    )
```
